128 devices in a mesh: tm: 32 (over y_lo, z, x), row: 4 (over y_hi, core).
Axes of the slice: x: 4, y: 4 (y_hi: 2, y_lo: 2; y = y_hi * 2 + y_lo), z: 4, core: 2. Of those that a mesh axis runs over, the one named last changes fastest.
Arguments:
- inputs: bfloat16 [1, 2048, 16, 16, 256], P(None, 'tm', 'row'), may hold values from -6 to 6
- decays: float32 [2048, 256], P('tm'), may hold values from 0.4 to 0.999999, as said below
- in_kernel: bfloat16 [3, 3, 256, 256], replicated, may hold values from -0.125 to 0.125
- out_kernel: bfloat16 [3, 3, 256, 256], replicated, may hold values from -0.125 to 0.125
- skip: float32 [256], replicated, may hold values from -1 to 1
- cotangent: bfloat16 [1, 2048, 16, 16, 256], P(None, 'tm', 'row'), may hold values from -6 to 6
Outputs:
- outputs: bfloat16 [1, 2048, 16, 16, 256], P(None, 'tm', 'row')
- in_kernel_grad: float32 [3, 3, 256, 256], replicated
- out_kernel_grad: float32 [3, 3, 256, 256], replicated
The draws below stay inside these ranges and needn't reach their ends.
Inputs may be any that keep to these rules, and one draw needn't show every extreme that they name: `decays`: strictly below one.
All inputs are finite; a program needn't handle non-finite values.
Results may differ from the reference program's by a relative error of at most 0.0043.
Values may be sent and summed in bfloat16 or wider, within the bound.
A program may use at most 128 MiB of HBM per device.

```python
import math
import jax
import jax.numpy as jnp
from jax import lax

C = 256
P_SIZE = 256
WD = 16
CLIPS = 1
SEGMENT_LENGTH = 2048
H = 16


def draw_decays(key, part):
    sampler_seeds = jax.random.split(key, 6)
    slow_share = 0.55
    is_slow = jax.random.bernoulli(sampler_seeds[0], slow_share, (P_SIZE,))
    slower_decay_rate = jax.random.uniform(sampler_seeds[1], (P_SIZE,), jnp.float32, 0.1, 0.6) / SEGMENT_LENGTH
    fast_rate = jnp.exp(jax.random.uniform(sampler_seeds[2], (P_SIZE,), jnp.float32, math.log(0.02), math.log(0.1)))
    base_rate = jnp.where(is_slow, slower_decay_rate, fast_rate)
    modulation = jnp.exp(jax.random.uniform(sampler_seeds[3], (SEGMENT_LENGTH, 1), jnp.float32, math.log(0.5), math.log(2.0)))
    spike_indices = jax.random.randint(sampler_seeds[4], (3,), 0, SEGMENT_LENGTH)
    marked_timesteps = jnp.any(jnp.arange(SEGMENT_LENGTH)[:, None] == spike_indices[None, :], axis=1)
    spike_amplitude = jax.random.uniform(sampler_seeds[5], (SEGMENT_LENGTH, 1), jnp.float32, 0.6, 0.85)
    gain_factor = jnp.where(marked_timesteps[:, None], spike_amplitude, 1.0)
    return jnp.minimum(jnp.exp(-base_rate[None, :] * modulation) * gain_factor, 0.999999)


def shard_levels(key, shape, cuts, low, largest):
    def one(dim, blocks):
        draws = jax.random.uniform(jax.random.fold_in(jax.random.fold_in(key, 6), dim), (blocks,), jnp.float32, low / len(cuts), largest / len(cuts))
        return jnp.repeat(jnp.exp(draws), shape[dim] // blocks).reshape((-1,) + (1,) * (len(shape) - dim - 1))

    gain = one(*cuts[0])
    for cut in cuts[1:]:
        gain = gain * one(*cut)
    return gain


def normal_values(rng, dims, scale, bound, cuts=(), held_as=jnp.bfloat16):
    values = jax.random.normal(rng, dims, jnp.float32) * scale
    if len(cuts) > 0:
        values = shard_levels(rng, dims, cuts, -0.22, 0.18) * values
    return jnp.clip(values, min=-bound, max=bound).astype(held_as)


def setup_inputs(seed: int = 0) -> dict:
    key_list = jax.random.split(jax.random.key(seed), 7)
    return {
        "inputs": normal_values(key_list[0], (CLIPS, SEGMENT_LENGTH, H, WD, C), 1.0, 6.0, ((1, 32), (2, 4))),
        "decays": draw_decays(jax.random.fold_in(key_list[6], 71), 0),
        "in_kernel": normal_values(key_list[2], (3, 3, C, P_SIZE), (9 * C) ** -0.5, 0.125),
        "out_kernel": normal_values(key_list[3], (3, 3, P_SIZE, C), (9 * P_SIZE) ** -0.5, 0.125),
        "skip": jnp.clip(jax.random.uniform(key_list[4], (C,), jnp.float32, -1.0, 1.0), -1.0, 1.0),
        "cotangent": normal_values(key_list[5], (CLIPS, SEGMENT_LENGTH, H, WD, C), 1.0, 6.0, ((1, 32), (2, 4))),
    }


def conv_same(field, kernel):
    return lax.conv_general_dilated(field.astype(jnp.float32), kernel.astype(jnp.float32), (1, 1), ((1, 1), (1, 1)), dimension_numbers=('NHWC', 'HWIO', 'NHWC'), precision=lax.Precision.HIGHEST)

def tap_grads(field, cotan_field):
    height = cotan_field.shape[1]
    width = cotan_field.shape[2]
    padded = jnp.pad(field.astype(jnp.float32), ((0, 0), (1, 1), (1, 1), (0, 0)))
    cotan_wide = cotan_field.astype(jnp.float32)
    collected = []
    for tap_row in range(3):
        for tap_col in range(3):
            window = padded[:, tap_row:tap_row + height, tap_col:tap_col + width, :]
            collected.append(jnp.einsum('bhwi,bhwo->io', window, cotan_wide, precision=lax.Precision.HIGHEST))
    return jnp.stack(collected).reshape(3, 3, field.shape[3], cotan_field.shape[3])

def reference(inputs, decays, in_kernel, out_kernel, skip, cotangent):
    batch_rows = CLIPS * SEGMENT_LENGTH
    flat_in = inputs.reshape(batch_rows, H, WD, C)
    drive = conv_same(flat_in, in_kernel).reshape(CLIPS, SEGMENT_LENGTH, H, WD, P_SIZE)
    scale_in = jnp.sqrt((1.0 - decays) * (1.0 + decays))

    def forward_step(carry, entries):
        decay_row, scale_row, drive_row = entries
        updated = decay_row * carry + scale_row * drive_row
        return (updated, updated)
    start = jnp.zeros((CLIPS, H, WD, P_SIZE), jnp.float32)
    _, states = lax.scan(forward_step, start, (decays, scale_in, jnp.moveaxis(drive, 1, 0)))
    states = jnp.moveaxis(states, 0, 1)
    state_low = states.astype(jnp.bfloat16)
    flat_state = state_low.reshape(batch_rows, H, WD, P_SIZE)
    mixed_out = conv_same(flat_state, out_kernel).reshape(CLIPS, SEGMENT_LENGTH, H, WD, C)
    outputs = (mixed_out + skip * inputs.astype(jnp.float32)).astype(jnp.bfloat16)
    grad_scale = 1.0 / math.sqrt(CLIPS * SEGMENT_LENGTH * H * WD)
    flat_cot = cotangent.reshape(batch_rows, H, WD, C)
    out_kernel_grad = tap_grads(flat_state, flat_cot) * grad_scale
    flipped = jnp.transpose(jnp.flip(out_kernel, (0, 1)), (0, 1, 3, 2))
    state_cot = conv_same(flat_cot, flipped).reshape(CLIPS, SEGMENT_LENGTH, H, WD, P_SIZE)
    next_decay = jnp.concatenate([decays[1:], jnp.ones_like(decays[:1])], axis=0)

    def backward_step(carry, entries):
        decay_row, cot_row = entries
        updated = cot_row + decay_row * carry
        return (updated, updated)
    _, adjoint = lax.scan(backward_step, start, (next_decay, jnp.moveaxis(state_cot, 1, 0)), reverse=True)
    adjoint = jnp.moveaxis(adjoint, 0, 1)
    drive_cot = (scale_in[None, :, None, None, :] * adjoint).astype(jnp.bfloat16)
    in_kernel_grad = tap_grads(flat_in, drive_cot.reshape(batch_rows, H, WD, P_SIZE)) * grad_scale
    return (outputs, in_kernel_grad, out_kernel_grad)
```

```python
import functools
import math

import jax
import jax.numpy as jnp
from jax import lax
from jax.experimental import pallas as pl
from jax.experimental.pallas import tpu as pltpu
from jax.sharding import PartitionSpec as P

MESH = pl.DeviceIdType.MESH
F32 = jnp.float32
BF16 = jnp.bfloat16

T = 64
R = 4
W = 16
CH = 256
FB = 16
NB = T // FB
M = FB * W
CELLS = R * W
MSG = CELLS + 8
HALF = 9 * 128
ORDERS = (("x", "z", "y"), ("z", "y", "x"), ("y", "x", "z"))


def column(rows):
    return lax.broadcasted_iota(jnp.int32, (rows, CH), 0) & (W - 1)


def from_left(v):
    return jnp.where(column(v.shape[0]) == 0, 0.0, pltpu.roll(v, 1, 0))


def from_right(v):
    return jnp.where(column(v.shape[0]) == W - 1, 0.0, pltpu.roll(v, v.shape[0] - 1, 0))


def kernel(
    grad_scale,
    x_hbm, dec, kin_hbm, kout_hbm, skip, cot_hbm,
    out_hbm, gin_hbm, gout_hbm,
    xi, ci, kin, kout, ft, drv, adj, sb, dcb, ob, sc,
    rx, rz, ry, incoming,
    acc, gbuf, psend, precv, hbuf, s1, r1, c1, r2, c2, r3, agb, pgb, fb,
    lsem, wsem, osem, gsem,
    hsend, hrecv, xsend, xrecv, zsend, zrecv, ysend, yrecv,
    psem, prem, s1s, s1r, s2s, s2r, s3s, s3r, a2s, a2r, a1s, a1r, pgs, pgr,
):
    tm = lax.axis_index("tm")
    row = lax.axis_index("row")
    core = lax.rem(row, 2)
    y_lo = tm // 16
    pos = {"x": lax.rem(tm, 4), "z": lax.rem(tm // 4, 4), "y": (row // 2) * 2 + y_lo}

    def mate(axis, k):
        if axis == "x":
            return ((tm // 4) * 4 + k, row)
        if axis == "z":
            return (y_lo * 16 + k * 4 + lax.rem(tm, 4), row)
        return (lax.rem(k, 2) * 16 + lax.rem(tm, 16), (k // 2) * 2 + core)

    def step(axis, d):
        return lax.rem(pos[axis] + d, 4)

    pair = (tm, row + 1 - 2 * core)
    up = (tm, row - 1)
    down = (tm, row + 1)

    def remote(src, dst, ssem, rsem, device):
        return pltpu.make_async_remote_copy(
            src_ref=src, dst_ref=dst, send_sem=ssem, recv_sem=rsem,
            device_id=device, device_id_type=MESH,
        )

    mid = pl.ds(CH, CH)
    loads = []
    for r in range(R):
        for n, (hbm, buf) in enumerate(((x_hbm, xi), (cot_hbm, ci))):
            loads.append(pltpu.make_async_copy(hbm.at[:, r], buf.at[r + 1, :, :, mid], lsem.at[n, r]))
    load_kin = pltpu.make_async_copy(kin_hbm, kin, wsem.at[0])
    load_kout = pltpu.make_async_copy(kout_hbm, kout, wsem.at[1])
    load_kout.start()
    for load in loads:
        load.start()
    load_kin.start()

    barrier = pltpu.get_barrier_semaphore()
    for axis in ("x", "z", "y"):
        for d in (1, 2, 3):
            pl.semaphore_signal(barrier, inc=1, device_id=mate(axis, step(axis, d)), device_id_type=MESH)
    pl.semaphore_signal(barrier, inc=1, device_id=pair, device_id_type=MESH)

    @pl.when(row == 1)
    def _():
        pl.semaphore_signal(barrier, inc=1, device_id=down, device_id_type=MESH)
        pl.semaphore_wait(barrier, 11)

    @pl.when(row == 2)
    def _():
        pl.semaphore_signal(barrier, inc=1, device_id=up, device_id_type=MESH)
        pl.semaphore_wait(barrier, 11)

    @pl.when((row == 0) | (row == 3))
    def _():
        pl.semaphore_wait(barrier, 10)

    def halo(n, way):
        if n == 2:
            src = sb.at[1] if way == 0 else sb.at[R]
            dst = sb.at[R + 1] if way == 0 else sb.at[0]
        else:
            hbm, buf = ((x_hbm, xi), (cot_hbm, ci))[n]
            src = hbm.at[:, 0] if way == 0 else hbm.at[:, R - 1]
            dst = buf.at[R + 1, :, :, mid] if way == 0 else buf.at[0, :, :, mid]
        return remote(src, dst, hsend.at[n, way], hrecv.at[n, way], up if way == 0 else down)

    def halo_start(n):
        @pl.when(row > 0)
        def _():
            halo(n, 0).start()

        @pl.when(row < 3)
        def _():
            halo(n, 1).start()

    def halo_arrived(n):
        @pl.when(row < 3)
        def _():
            halo(n, 0).wait_recv()

        @pl.when(row > 0)
        def _():
            halo(n, 1).wait_recv()

    def halo_sent(n):
        @pl.when(row > 0)
        def _():
            halo(n, 0).wait_send()

        @pl.when(row < 3)
        def _():
            halo(n, 1).wait_send()

    halo_start(0)
    halo_start(1)

    for at, edge in ((0, 0), (3, R + 1)):
        @pl.when(row == at)
        def _():
            zero = jnp.zeros((T, W, CH), BF16)
            xi[edge, :, :, CH:2 * CH] = zero
            ci[edge, :, :, CH:2 * CH] = zero
            sb[edge] = zero

    d_all = dec[...]
    sc[...] = jnp.sqrt((1.0 - d_all) * (1.0 + d_all))

    load_kout.wait()
    for i in range(3):
        for j in range(3):
            ft[(i * 3 + j) * CH:(i * 3 + j + 1) * CH, :] = kout[2 - i, 2 - j].T

    def widen(buf, r):
        def body(b, _):
            f0 = b * FB
            v = buf[r, pl.ds(f0, FB), :, CH:2 * CH].reshape(M, CH).astype(F32)
            buf[r, pl.ds(f0, FB), :, 0:CH] = from_left(v).astype(BF16).reshape(FB, W, CH)
            buf[r, pl.ds(f0, FB), :, 2 * CH:3 * CH] = from_right(v).astype(BF16).reshape(FB, W, CH)
            return 0

        lax.fori_loop(0, NB, body, 0)

    def conv(buf, weights, dst, first, stride, count):
        def body(n, _):
            h = first + (n // NB) * stride
            f0 = lax.rem(n, NB) * FB
            lhs = jnp.concatenate(
                [buf[h + i, pl.ds(f0, FB)].reshape(M, 3 * CH) for i in range(3)], axis=1
            )
            dst[h, pl.ds(f0, FB)] = jnp.dot(lhs, weights[...], preferred_element_type=F32).reshape(FB, W, CH)
            return 0

        lax.fori_loop(0, count * NB, body, 0)

    for n, load in enumerate(loads):
        load.wait()
    def widen_own(r, _):
        widen(xi, r)
        widen(ci, r)
        return 0

    lax.fori_loop(1, R + 1, widen_own, 0)
    load_kin.wait()
    conv(xi, kin, drv, 1, 1, 2)
    conv(ci, ft, adj, 1, 1, 2)
    halo_arrived(0)
    widen(xi, 0)
    widen(xi, R + 1)
    conv(xi, kin, drv, 0, 3, 2)

    UN = 4

    def decay_at(t):
        return dec[pl.ds(t, 1), :]

    def ends_forward(n, carry):
        state, prod = carry
        for u in range(UN):
            t = n * UN + u
            d = decay_at(t)
            state = d * state + sc[pl.ds(t, 1), :] * drv[:, t]
            prod = prod * d
        return state, prod

    def ends_backward(n, v):
        for u in range(UN):
            t = T - 1 - (n * UN + u)
            v = decay_at(t) * (adj[:, t] + v)
        return v

    zero_state = jnp.zeros((R, W, CH), F32)

    def broadcast_line(buf, way, axis, ssem, rsem, start):
        me = pos[axis]
        for d in (1, 2, 3):
            k = step(axis, d)
            if start:
                remote(buf.at[way, me], buf.at[way, me], ssem.at[way, d - 1], rsem.at[way, me], mate(axis, k)).start()
            else:
                copy = remote(buf.at[way, me], buf.at[way, k], ssem.at[way, d - 1], rsem.at[way, k], mate(axis, k))
                copy.wait()

    def fold(buf, way, axis):
        me = pos[axis]
        before = jnp.zeros((CELLS, CH), F32)
        before_decay = jnp.ones((1, CH), F32)
        total = before
        total_decay = before_decay
        for p in (range(4) if way == 0 else range(3, -1, -1)):
            e = buf[way, p, 0:CELLS]
            d = buf[way, p, CELLS:CELLS + 1]
            takes = (me > p) if way == 0 else (me < p)
            before = jnp.where(takes, d * before + e, before)
            before_decay = jnp.where(takes, before_decay * d, before_decay)
            total = d * total + e
            total_decay = total_decay * d
        return before, before_decay, total, total_decay

    def put(buf, way, axis, total, decay):
        me = pos[axis]
        buf[way, me, 0:CELLS] = total
        buf[way, me, CELLS:MSG] = jnp.broadcast_to(decay, (8, CH))

    y_mate = mate("y", (row // 2) * 2 + 1 - y_lo)

    def y_copy(way):
        return remote(ry.at[way, 0], ry.at[way, 1], ysend.at[way], yrecv.at[way], y_mate)

    def send_y(way):
        @pl.when(y_lo == way)
        def _():
            y_copy(way).start()

    def take_y(way, z_before, z_decay, x_before, x_decay):
        incoming[way] = x_decay * z_before + x_before

        @pl.when(y_lo == 1 - way)
        def _():
            y_copy(way).wait_recv()
            incoming[way] = x_decay * (z_decay * ry[way, 1] + z_before) + x_before

    end, decay = lax.fori_loop(0, T // UN, ends_forward, (zero_state, jnp.ones((1, CH), F32)))
    put(rx, 0, "x", end.reshape(CELLS, CH), decay)
    broadcast_line(rx, 0, "x", xsend, xrecv, True)

    halo_arrived(1)
    widen(ci, 0)
    widen(ci, R + 1)
    conv(ci, ft, adj, 0, 3, 2)
    lead = lax.fori_loop(0, T // UN, ends_backward, zero_state)
    put(rx, 1, "x", lead.reshape(CELLS, CH), decay)
    broadcast_line(rx, 1, "x", xsend, xrecv, True)

    broadcast_line(rx, 0, "x", xsend, xrecv, False)
    fx, fxd, total, total_decay = fold(rx, 0, "x")
    put(rz, 0, "z", total, total_decay)
    broadcast_line(rz, 0, "z", zsend, zrecv, True)

    broadcast_line(rx, 1, "x", xsend, xrecv, False)
    bx, bxd, total, total_decay = fold(rx, 1, "x")
    put(rz, 1, "z", total, total_decay)
    broadcast_line(rz, 1, "z", zsend, zrecv, True)

    broadcast_line(rz, 0, "z", zsend, zrecv, False)
    fz, fzd, total, _ = fold(rz, 0, "z")
    ry[0, 0] = total
    send_y(0)
    broadcast_line(rz, 1, "z", zsend, zrecv, False)
    bz, bzd, total, _ = fold(rz, 1, "z")
    ry[1, 0] = total
    send_y(1)

    take_y(0, fz, fzd, fx, fxd)

    def states(n, state):
        for u in range(UN):
            t = n * UN + u
            state = decay_at(t) * state + sc[pl.ds(t, 1), :] * drv[:, t]
            sb[1:R + 1, t] = state.astype(BF16)
        return state

    lax.fori_loop(0, T // UN, states, incoming[0].reshape(R, W, CH))
    halo_start(2)
    take_y(1, bz, bzd, bx, bxd)

    def grad_rows(field, other, other_at):
        def body(h, _):
            turned = field[h + other_at].reshape(T * W, CH).T
            for i in range(3):
                acc[i] += jnp.dot(turned, other[h + i].reshape(T * W, 3 * CH), preferred_element_type=F32)
            return 0
        return body

    def adjoints(n, v):
        for u in range(UN):
            t = T - 1 - (n * UN + u)
            a = adj[:, t] + v
            dcb[:, t] = (sc[pl.ds(t, 1), :] * a).astype(BF16)
            v = decay_at(t) * a
        return v

    def reduction(g):
        mine = pl.ds(0, 1)
        pair_copy = remote(psend.at[g], precv.at[g], psem.at[g], prem.at[g], pair)

        def begin():
            for i in range(3):
                for j in range(3):
                    n = i * 3 + j
                    if g == 0:
                        v = acc[2 - i, :, (2 - j) * CH:(3 - j) * CH]
                    else:
                        v = acc[i, :, j * CH:(j + 1) * CH].T
                    gbuf[0, n * 128:(n + 1) * 128, :] = v[0:128]
                    gbuf[1, n * 128:(n + 1) * 128, :] = v[128:256]
            psend[g] = gbuf[1 - core].astype(BF16)
            pair_copy.start()

        def first():
            pair_copy.wait()
            for q in range(3):
                for k in range(4):
                    at = q * 384 + k * 96
                    v = gbuf[core, at:at + 96, :] + precv[g, at:at + 96, :].astype(F32)
                    hbuf[q, k] = v
                    s1[g, q, k] = v.astype(BF16)
            for q in range(3):
                for d in (1, 2, 3):
                    k = step(ORDERS[q][0], d)
                    remote(s1.at[g, q, k], r1.at[g, q, d - 1], s1s.at[g, q, d - 1], s1r.at[g, q, d - 1],
                           mate(ORDERS[q][0], k)).start()

        def second():
            for q in range(3):
                axis = ORDERS[q][0]
                total = hbuf[q, pos[axis]]
                for d in (1, 2, 3):
                    k = step(axis, d)
                    remote(s1.at[g, q, k], r1.at[g, q, d - 1], s1s.at[g, q, d - 1], s1r.at[g, q, d - 1],
                           mate(axis, k)).wait()
                    total = total + r1[g, q, d - 1].astype(F32)
                for k in range(4):
                    c1[g, q, k] = total[48 * (k // 2):48 * (k // 2) + 48, 128 * (k % 2):128 * (k % 2) + 128]
                axis = ORDERS[q][1]
                for d in (1, 2, 3):
                    k = step(axis, d)
                    remote(c1.at[g, q, k], r2.at[g, q, d - 1], s2s.at[g, q, d - 1], s2r.at[g, q, d - 1],
                           mate(axis, k)).start()

        def third():
            for q in range(3):
                axis = ORDERS[q][1]
                total = c1[g, q, pos[axis]]
                for d in (1, 2, 3):
                    k = step(axis, d)
                    remote(c1.at[g, q, k], r2.at[g, q, d - 1], s2s.at[g, q, d - 1], s2r.at[g, q, d - 1],
                           mate(axis, k)).wait()
                    total = total + r2[g, q, d - 1]
                c2[g, q] = total
                axis = ORDERS[q][2]
                for d in (1, 2, 3):
                    remote(c2.at[g, q], r3.at[g, q, d - 1], s3s.at[g, q, d - 1], s3r.at[g, q, d - 1],
                           mate(axis, step(axis, d))).start()

        def spread_copy(q, d, arriving):
            axis = ORDERS[q][1]
            k1 = pos[ORDERS[q][0]]
            k2 = lax.rem(pos[axis] + 4 - d, 4) if arriving else pos[axis]
            return remote(agb.at[g, q, k1, k2], agb.at[g, q, k1, k2], a2s.at[g, q, d - 1], a2r.at[g, q, d - 1],
                          mate(axis, step(axis, d)))

        def wide_copy(q, d, arriving):
            axis = ORDERS[q][0]
            k1 = lax.rem(pos[axis] + 4 - d, 4) if arriving else pos[axis]
            return remote(agb.at[g, q, k1], agb.at[g, q, k1], a1s.at[g, q, d - 1], a1r.at[g, q, d - 1],
                          mate(axis, step(axis, d)))

        def hand_over(q, d):
            k1 = lax.rem(pos[ORDERS[q][0]] + 4 - d, 4)
            return remote(agb.at[g, q, k1], pgb.at[g, q, k1], pgs.at[g, q, d], pgr.at[g, q, d], pair)

        def fourth():
            for q in range(3):
                axis = ORDERS[q][2]
                for d in (1, 2, 3):
                    remote(c2.at[g, q], r3.at[g, q, d - 1], s3s.at[g, q, d - 1], s3r.at[g, q, d - 1],
                           mate(axis, step(axis, d))).wait()
                total = (c2[g, q] + r3[g, q, 1]) + (r3[g, q, 0] + r3[g, q, 2])
                agb[g, q, pos[ORDERS[q][0]], pos[ORDERS[q][1]]] = (total * grad_scale).astype(BF16)
                for d in (1, 2, 3):
                    spread_copy(q, d, False).start()

        def fifth():
            for q in range(3):
                for d in (1, 2, 3):
                    spread_copy(q, d, True).wait_recv()
                    spread_copy(q, d, False).wait_send()
                for d in (1, 2, 3):
                    wide_copy(q, d, False).start()
                hand_over(q, 0).start()

        def sixth():
            for d in (1, 2, 3):
                for q in range(3):
                    wide_copy(q, d, True).wait_recv()
                    wide_copy(q, d, False).wait_send()
                    hand_over(q, d).start()

        out = pltpu.make_async_copy(fb.at[g], (gout_hbm, gin_hbm)[g], gsem.at[g])

        def last():
            for q in range(3):
                for d in range(4):
                    hand_over(q, d).wait()
            for q in range(3):
                for k1 in range(4):
                    for k2 in range(4):
                        at = q * 384 + k1 * 96 + 48 * (k2 // 2)
                        lanes = slice(128 * (k2 % 2), 128 * (k2 % 2) + 128)
                        fb[g, core, at:at + 48, lanes] = agb[g, q, k1, k2]
                        fb[g, 1 - core, at:at + 48, lanes] = pgb[g, q, k1, k2]
            out.start()

        return [begin, first, second, third, fourth, fifth, sixth, last], out

    stages_out, done_out = reduction(0)
    stages_in, done_in = reduction(1)

    acc[...] = jnp.zeros_like(acc)
    lax.fori_loop(0, R, grad_rows(sb, ci, 1), 0)
    stages_out[0]()
    lax.fori_loop(0, T // UN, adjoints, incoming[1].reshape(R, W, CH))
    stages_out[1]()
    acc[...] = jnp.zeros_like(acc)
    body = grad_rows(dcb, xi, 0)
    lax.fori_loop(0, 2, body, 0)
    stages_out[2]()
    lax.fori_loop(2, 4, body, 0)
    stages_in[0]()
    stages_out[3]()
    halo_arrived(2)

    def mix(h):
        def block(b, _):
            f0 = b * FB
            lhs = jnp.concatenate([sb[h + i, pl.ds(f0, FB)].reshape(M, CH) for i in range(3)], axis=1)
            parts = []
            for j in range(3):
                weights = jnp.concatenate([kout[i, j] for i in range(3)], axis=0)
                parts.append(jnp.dot(lhs, weights, preferred_element_type=F32))
            x = xi[h + 1, pl.ds(f0, FB), :, CH:2 * CH].reshape(M, CH).astype(F32)
            y = from_left(parts[0]) + parts[1] + from_right(parts[2]) + skip[...] * x
            ob[h, pl.ds(f0, FB)] = y.astype(BF16).reshape(FB, W, CH)
            return 0

        lax.fori_loop(0, NB, block, 0)
        store = pltpu.make_async_copy(ob.at[h], out_hbm.at[:, h], osem.at[h])
        store.start()
        return store

    stages_in[1]()
    stores = [mix(0)]
    stages_out[4]()
    stages_in[2]()
    stores.append(mix(1))
    stages_out[5]()
    stages_in[3]()
    stores.append(mix(2))
    stages_out[6]()
    stages_in[4]()
    stores.append(mix(3))
    stages_in[5]()
    stages_out[7]()
    stages_in[6]()
    stages_in[7]()

    for n in range(3):
        halo_sent(n)
    for way in range(2):
        @pl.when(y_lo == way)
        def _():
            y_copy(way).wait_send()
    for store in stores:
        store.wait()
    done_out.wait()
    done_in.wait()


def per_device(inputs, decays, in_kernel, out_kernel, skip, cotangent):
    cells_all = T * lax.axis_size("tm") * R * lax.axis_size("row") * W
    grad_scale = 1.0 / math.sqrt(cells_all)
    anywhere = pl.BlockSpec(memory_space=pl.ANY)
    vmem = pl.BlockSpec(memory_space=pltpu.VMEM)
    dma = pltpu.SemaphoreType.DMA
    V = pltpu.VMEM
    half = jax.ShapeDtypeStruct((2, HALF, CH), BF16)
    outputs, in_grad, out_grad = pl.pallas_call(
        functools.partial(kernel, grad_scale),
        out_shape=(jax.ShapeDtypeStruct((T, R, W, CH), BF16), half, half),
        in_specs=[anywhere, vmem, anywhere, anywhere, vmem, anywhere],
        out_specs=(anywhere, anywhere, anywhere),
        scratch_shapes=[
            V((R + 2, T, W, 3 * CH), BF16),
            V((R + 2, T, W, 3 * CH), BF16),
            V((9 * CH, CH), BF16),
            V((3, 3, CH, CH), BF16),
            V((9 * CH, CH), BF16),
            V((R, T, W, CH), F32),
            V((R, T, W, CH), F32),
            V((R + 2, T, W, CH), BF16),
            V((R, T, W, CH), BF16),
            V((R, T, W, CH), BF16),
            V((T, CH), F32),
            V((2, 4, MSG, CH), F32),
            V((2, 4, MSG, CH), F32),
            V((2, 2, CELLS, CH), F32),
            V((2, CELLS, CH), F32),
            V((3, CH, 3 * CH), F32),
            V((2, HALF, CH), F32),
            V((2, HALF, CH), BF16),
            V((2, HALF, CH), BF16),
            V((3, 4, 96, CH), F32),
            V((2, 3, 4, 96, CH), BF16),
            V((2, 3, 3, 96, CH), BF16),
            V((2, 3, 4, 48, 128), F32),
            V((2, 3, 3, 48, 128), F32),
            V((2, 3, 48, 128), F32),
            V((2, 3, 3, 48, 128), F32),
            V((2, 3, 4, 4, 48, 128), BF16),
            V((2, 3, 4, 4, 48, 128), BF16),
            V((2, 2, HALF, CH), BF16),
            dma((2, R)), dma((2,)), dma((R,)), dma((2,)),
            dma((3, 2)), dma((3, 2)),
            dma((2, 3)), dma((2, 4)), dma((2, 3)), dma((2, 4)), dma((2,)), dma((2,)),
            dma((2,)), dma((2,)),
            dma((2, 3, 3)), dma((2, 3, 3)), dma((2, 3, 3)), dma((2, 3, 3)), dma((2, 3, 3)), dma((2, 3, 3)),
            dma((2, 3, 3)), dma((2, 3, 3)), dma((2, 3, 3)), dma((2, 3, 3)),
            dma((2, 3, 4)), dma((2, 3, 4)),
        ],
        compiler_params=pltpu.CompilerParams(
            collective_id=0, has_side_effects=True, vmem_limit_bytes=62 * 1024 * 1024
        ),
    )(
        inputs.reshape(T, R, W, CH), decays, in_kernel.reshape(9 * CH, CH), out_kernel,
        skip.reshape(1, CH), cotangent.reshape(T, R, W, CH),
    )

    def whole(halves):
        return halves.reshape(2, 9, 128, CH).transpose(1, 0, 2, 3).reshape(3, 3, CH, CH).astype(F32)

    return outputs.reshape(inputs.shape), whole(in_grad), whole(out_grad)


def solution(mesh):
    return jax.shard_map(
        per_device,
        mesh=mesh,
        in_specs=(
            P(None, "tm", "row", None, None),
            P("tm", None),
            P(),
            P(),
            P(),
            P(None, "tm", "row", None, None),
        ),
        out_specs=(P(None, "tm", "row", None, None), P(), P()),
        check_vma=False,
    )
```

```python
import functools
import math

import jax
import jax.numpy as jnp
from jax import lax
from jax.experimental import pallas as pl
from jax.experimental.pallas import tpu as pltpu
from jax.sharding import PartitionSpec as P

MESH = pl.DeviceIdType.MESH
F32 = jnp.float32
BF16 = jnp.bfloat16

T = 64
R = 4
W = 16
CH = 256
FB = 32
NB = T // FB
M = FB * W
CELLS = R * W
MSG = CELLS + 8
LINE = 4
CHUNK = (48, 128)
ORDERS = (("x", "z", "y"), ("z", "y", "x"), ("y", "x", "z"))


def column(rows):
    return lax.broadcasted_iota(jnp.int32, (rows, CH), 0) & (W - 1)


def from_left(v):
    return jnp.where(column(v.shape[0]) == 0, 0.0, pltpu.roll(v, 1, 0))


def from_right(v):
    return jnp.where(column(v.shape[0]) == W - 1, 0.0, pltpu.roll(v, v.shape[0] - 1, 0))


def kernel(
    grad_scale,
    x_hbm, dec, kin_hbm, kout_hbm, skip, cot_hbm,
    out_hbm, gin_hbm, gout_hbm,
    xi, ci, kin, kout, ft, drv, adj, sb, dcb, ob, sc,
    rx, rz, ry, incoming,
    turned, acc, psend, precv, h1, h2, own, s1, r1, c1, r2, c2, r3, agb, pgb, fb,
    lsem, wsem, osem, gsem,
    hsend, hrecv, xsend, xrecv, zsend, zrecv, ysend, yrecv,
    psem, prem, s1s, s1r, s2s, s2r, s3s, s3r, a2s, a2r, a1s, a1r, pgs, pgr,
):
    tm = lax.axis_index("tm")
    row = lax.axis_index("row")
    core = lax.rem(row, 2)
    y_lo = tm // 16
    pos = {"x": lax.rem(tm, 4), "z": lax.rem(tm // 4, 4), "y": (row // 2) * 2 + y_lo}

    def mate(axis, k):
        if axis == "x":
            return ((tm // 4) * 4 + k, row)
        if axis == "z":
            return (y_lo * 16 + k * 4 + lax.rem(tm, 4), row)
        return (lax.rem(k, 2) * 16 + lax.rem(tm, 16), (k // 2) * 2 + core)

    def mates(axis):
        return [mate(axis, lax.rem(pos[axis] + d, LINE)) for d in (1, 2, 3)]

    pair = (tm, row + 1 - 2 * core)
    up = (tm, row - 1)
    down = (tm, row + 1)

    def remote(src, dst, ssem, rsem, device):
        return pltpu.make_async_remote_copy(
            src_ref=src, dst_ref=dst, send_sem=ssem, recv_sem=rsem,
            device_id=device, device_id_type=MESH,
        )

    barrier = pltpu.get_barrier_semaphore()

    def greet(device):
        pl.semaphore_signal(barrier, inc=1, device_id=device, device_id_type=MESH)

    @pl.when(row == 1)
    def _():
        greet(down)

    @pl.when(row == 2)
    def _():
        greet(up)

    greet(pair)
    for axis in ("y", "x", "z"):
        for device in mates(axis):
            greet(device)

    mid = pl.ds(CH, CH)
    loads = [
        [
            pltpu.make_async_copy(hbm.at[:, r], buf.at[r + 1, :, :, mid], lsem.at[n, r])
            for r in range(R)
        ]
        for n, (hbm, buf) in enumerate(((x_hbm, xi), (cot_hbm, ci)))
    ]
    load_kin = pltpu.make_async_copy(kin_hbm, kin, wsem.at[0])
    load_kout = pltpu.make_async_copy(kout_hbm, kout, wsem.at[1])
    for load in loads[0]:
        load.start()
    load_kin.start()
    load_kout.start()
    for load in loads[1]:
        load.start()

    for at, edge in ((0, 0), (3, R + 1)):
        @pl.when(row == at)
        def _():
            zero = jnp.zeros((T, W, CH), BF16)
            xi[edge, :, :, CH:2 * CH] = zero
            ci[edge, :, :, CH:2 * CH] = zero
            sb[edge] = zero

    d_all = dec[...]
    sc[...] = jnp.sqrt((1.0 - d_all) * (1.0 + d_all))

    @pl.when((row == 1) | (row == 2))
    def _():
        pl.semaphore_wait(barrier, 11)

    @pl.when((row == 0) | (row == 3))
    def _():
        pl.semaphore_wait(barrier, 10)

    def halo(n, way):
        if n == 2:
            src = sb.at[1] if way == 0 else sb.at[R]
            dst = sb.at[R + 1] if way == 0 else sb.at[0]
        else:
            hbm, buf = ((x_hbm, xi), (cot_hbm, ci))[n]
            src = hbm.at[:, 0] if way == 0 else hbm.at[:, R - 1]
            dst = buf.at[R + 1, :, :, mid] if way == 0 else buf.at[0, :, :, mid]
        return remote(src, dst, hsend.at[n, way], hrecv.at[n, way], up if way == 0 else down)

    def halo_start(n):
        @pl.when(row > 0)
        def _():
            halo(n, 0).start()

        @pl.when(row < 3)
        def _():
            halo(n, 1).start()

    def halo_arrived(n):
        @pl.when(row < 3)
        def _():
            halo(n, 0).wait_recv()

        @pl.when(row > 0)
        def _():
            halo(n, 1).wait_recv()

    def halo_sent(n):
        @pl.when(row > 0)
        def _():
            halo(n, 0).wait_send()

        @pl.when(row < 3)
        def _():
            halo(n, 1).wait_send()

    halo_start(0)
    halo_start(1)

    def widen(buf, r):
        def body(b, _):
            f0 = b * FB
            v = buf[r, pl.ds(f0, FB), :, CH:2 * CH].reshape(M, CH).astype(F32)
            buf[r, pl.ds(f0, FB), :, 0:CH] = from_left(v).astype(BF16).reshape(FB, W, CH)
            buf[r, pl.ds(f0, FB), :, 2 * CH:3 * CH] = from_right(v).astype(BF16).reshape(FB, W, CH)
            return 0

        lax.fori_loop(0, NB, body, 0)

    def conv(buf, weights, dst, first, stride, count):
        def body(n, _):
            h = first + (n // NB) * stride
            f0 = lax.rem(n, NB) * FB
            lhs = jnp.concatenate(
                [buf[h + i, pl.ds(f0, FB)].reshape(M, 3 * CH) for i in range(3)], axis=1
            )
            dst[h, pl.ds(f0, FB)] = jnp.dot(lhs, weights[...], preferred_element_type=F32).reshape(FB, W, CH)
            return 0

        lax.fori_loop(0, count * NB, body, 0)

    def turn_kernel():
        for i in range(3):
            for j in range(3):
                ft[(i * 3 + j) * CH:(i * 3 + j + 1) * CH, :] = kout[2 - i, 2 - j].T

    def widen_own(buf):
        def body(r, _):
            widen(buf, r)
            return 0

        lax.fori_loop(1, R + 1, body, 0)

    UN = 4

    def decay_at(t):
        return dec[pl.ds(t, 1), :]

    def ends_forward(n, carry):
        state, prod = carry
        for u in range(UN):
            t = n * UN + u
            d = decay_at(t)
            state = d * state + sc[pl.ds(t, 1), :] * drv[:, t]
            prod = prod * d
        return state, prod

    def ends_backward(n, v):
        for u in range(UN):
            t = T - 1 - (n * UN + u)
            v = decay_at(t) * (adj[:, t] + v)
        return v

    zero_state = jnp.zeros((R, W, CH), F32)

    def line(buf, way, axis, ssem, rsem, start):
        me = pos[axis]
        for d in (1, 2, 3):
            k = lax.rem(me + d, LINE)
            if start:
                remote(buf.at[way, me], buf.at[way, me], ssem.at[way, d - 1], rsem.at[way, me], mate(axis, k)).start()
            else:
                remote(buf.at[way, me], buf.at[way, k], ssem.at[way, d - 1], rsem.at[way, k], mate(axis, k)).wait()

    def fold(buf, way, me):
        before = jnp.zeros((CELLS, CH), F32)
        before_decay = jnp.ones((1, CH), F32)
        total = before
        total_decay = before_decay
        for p in (range(4) if way == 0 else range(3, -1, -1)):
            e, d = buf[way, p, 0:CELLS], buf[way, p, CELLS:CELLS + 1]
            takes = (me > p) if way == 0 else (me < p)
            before = jnp.where(takes, d * before + e, before)
            before_decay = jnp.where(takes, before_decay * d, before_decay)
            total = d * total + e
            total_decay = total_decay * d
        return before, before_decay, total, total_decay

    def put(buf, way, axis, total, decay):
        buf[way, pos[axis], 0:CELLS] = total
        buf[way, pos[axis], CELLS:MSG] = jnp.broadcast_to(decay, (8, CH))

    def y_copy(way):
        return remote(ry.at[way, 0], ry.at[way, 1], ysend.at[way], yrecv.at[way],
                      mate("y", (row // 2) * 2 + 1 - y_lo))

    def x_start(way, total, decay):
        put(rx, way, "x", total, decay)
        line(rx, way, "x", xsend, xrecv, True)

    def x_to_z(way):
        line(rx, way, "x", xsend, xrecv, False)
        before, before_decay, total, total_decay = fold(rx, way, pos["x"])
        put(rz, way, "z", total, total_decay)
        line(rz, way, "z", zsend, zrecv, True)
        return before, before_decay

    def z_to_y(way):
        line(rz, way, "z", zsend, zrecv, False)
        before, before_decay, total, _ = fold(rz, way, pos["z"])
        ry[way, 0] = total

        @pl.when(y_lo == way)
        def _():
            y_copy(way).start()

        return before, before_decay

    def from_y(way, z_side, x_side):
        z_before, z_decay = z_side
        x_before, x_decay = x_side
        incoming[way] = x_decay * z_before + x_before

        @pl.when(y_lo == 1 - way)
        def _():
            y_copy(way).wait_recv()
            incoming[way] = x_decay * (z_decay * ry[way, 1] + z_before) + x_before

    def states(n, state):
        for u in range(UN):
            t = n * UN + u
            state = decay_at(t) * state + sc[pl.ds(t, 1), :] * drv[:, t]
            sb[1:R + 1, t] = state.astype(BF16)
        return state

    for load in loads[0]:
        load.wait()
    widen_own(xi)
    load_kin.wait()
    conv(xi, kin, drv, 1, 1, 2)
    halo_arrived(0)
    widen(xi, 0)
    widen(xi, R + 1)
    conv(xi, kin, drv, 0, 3, 2)
    end, decay = lax.fori_loop(0, T // UN, ends_forward, (zero_state, jnp.ones((1, CH), F32)))
    x_start(0, end.reshape(CELLS, CH), decay)

    load_kout.wait()
    turn_kernel()
    for load in loads[1]:
        load.wait()
    widen_own(ci)
    conv(ci, ft, adj, 1, 1, 1)
    fx = x_to_z(0)
    conv(ci, ft, adj, 2, 1, 1)
    halo_arrived(1)
    widen(ci, 0)
    widen(ci, R + 1)
    conv(ci, ft, adj, 0, 1, 1)
    fz = z_to_y(0)
    conv(ci, ft, adj, 3, 1, 1)
    lead = lax.fori_loop(0, T // UN, ends_backward, zero_state)
    x_start(1, lead.reshape(CELLS, CH), decay)
    from_y(0, fz, fx)
    lax.fori_loop(0, T // UN, states, incoming[0].reshape(R, W, CH))
    halo_start(2)

    def turn(field, at):
        def body(h, _):
            turned[h] = field[h + at].reshape(T * W, CH).T
            return 0

        lax.fori_loop(0, R, body, 0)

    def row_tap(g, other, i):
        acc[g, i] = jnp.dot(turned[0], other[i].reshape(T * W, 3 * CH), preferred_element_type=F32)

        def body(h, _):
            acc[g, i] += jnp.dot(turned[h], other[h + i].reshape(T * W, 3 * CH), preferred_element_type=F32)
            return 0

        lax.fori_loop(1, R, body, 0)

    def adjoints(n, v):
        for u in range(UN):
            t = T - 1 - (n * UN + u)
            a = adj[:, t] + v
            dcb[:, t] = (sc[pl.ds(t, 1), :] * a).astype(BF16)
            v = decay_at(t) * a
        return v

    def part(g, q):
        pair_copy = remote(psend.at[g, q], precv.at[g, q], psem.at[g, q], prem.at[g, q], pair)

        def half(t, which):
            if g == 0:
                return acc[g, 2 - q, pl.ds(pl.multiple_of(which * 128, 128), 128), (2 - t) * CH:(3 - t) * CH]
            return acc[g, q, :, pl.ds(pl.multiple_of(t * CH + which * 128, 128), 128)].T

        def begin():
            for t in range(3):
                psend[g, q, t * 128:(t + 1) * 128] = half(t, 1 - core).astype(BF16)
            pair_copy.start()

        axis_1, axis_2, axis_3 = ORDERS[q]
        me_1, me_2 = pos[axis_1], pos[axis_2]

        def scatter():
            for t in range(3):
                h1[t * 128:(t + 1) * 128] = half(t, core)
            pair_copy.wait()
            for k in range(LINE):
                at = 96 * k
                v = h1[at:at + 96] + precv[g, q, at:at + 96].astype(F32)
                h2[k] = v
                s1[g, q, k] = v.astype(BF16)
            own[g, q] = h2[me_1]
            for d in (1, 2, 3):
                k = lax.rem(me_1 + d, LINE)
                remote(s1.at[g, q, k], r1.at[g, q, d - 1], s1s.at[g, q], s1r.at[g, q], mate(axis_1, k)).start()

        def second():
            remote(r1.at[g, q], r1.at[g, q], s1s.at[g, q], s1r.at[g, q], pair).wait()
            total = own[g, q]
            for d in range(3):
                total = total + r1[g, q, d].astype(F32)
            for k in range(LINE):
                c1[g, q, k] = total[48 * (k // 2):48 * (k // 2) + 48, 128 * (k % 2):128 * (k % 2) + 128]
            for d in (1, 2, 3):
                k = lax.rem(me_2 + d, LINE)
                remote(c1.at[g, q, k], r2.at[g, q, d - 1], s2s.at[g, q], s2r.at[g, q], mate(axis_2, k)).start()

        def cross():
            remote(r2.at[g, q], r2.at[g, q], s2s.at[g, q], s2r.at[g, q], pair).wait()
            c2[g, q] = c1[g, q, me_2] + r2[g, q, 0] + r2[g, q, 1] + r2[g, q, 2]
            for device, n in zip(mates(axis_3), range(3)):
                remote(c2.at[g, q], r3.at[g, q, n], s3s.at[g, q], s3r.at[g, q], device).start()

        def gather():
            remote(r3.at[g, q], r3.at[g, q], s3s.at[g, q], s3r.at[g, q], pair).wait()
            total = (c2[g, q] + r3[g, q, 1]) + (r3[g, q, 0] + r3[g, q, 2])
            mine = agb.at[g, q, me_1, me_2]
            mine[...] = (total * grad_scale).astype(BF16)
            for device in mates(axis_2):
                remote(mine, mine, a2s.at[g, q], a2r.at[g, q], device).start()

        def widen_out():
            three = agb.at[g, q, 0, pl.ds(0, 3)]
            remote(three, three, a2s.at[g, q], a2r.at[g, q], pair).wait()
            mine = agb.at[g, q, me_1]
            for device in mates(axis_1):
                remote(mine, mine, a1s.at[g, q], a1r.at[g, q], device).start()

        hand_over = remote(agb.at[g, q], pgb.at[g, q], pgs.at[g, q], pgr.at[g, q], pair)

        def share():
            three = agb.at[g, q, pl.ds(0, 3)]
            remote(three, three, a1s.at[g, q], a1r.at[g, q], pair).wait()
            hand_over.start()

        def unpack(buf, which):
            for k in range(LINE * LINE):
                at, lane = 48 * (k // 2), 128 * (k % 2)
                while at < 48 * (k // 2) + 48:
                    n = min(48 * (k // 2) + 48, (at // 128 + 1) * 128) - at
                    first = at - 48 * (k // 2)
                    fb[g, 3 * q + at // 128, which, at % 128:at % 128 + n, lane:lane + 128] = buf[g, q, k // LINE, k % LINE, first:first + n]
                    at += n

        def last():
            unpack(agb, core)
            hand_over.wait()
            unpack(pgb, 1 - core)
            out(g, q).start()

        return [begin, scatter, second, cross, gather, widen_out, share, last]

    def out(g, q):
        return pltpu.make_async_copy(
            fb.at[g, 3 * q:3 * q + 3], (gout_hbm, gin_hbm)[g].at[3 * q:3 * q + 3], gsem.at[g, q]
        )

    ro = [part(0, q) for q in range(3)]
    ri = [part(1, q) for q in range(3)]

    def run(*steps):
        for stages, n in steps:
            stages[n]()

    def mix(h):
        def block(b, _):
            f0 = b * FB
            lhs = jnp.concatenate([sb[h + i, pl.ds(f0, FB)].reshape(M, CH) for i in range(3)], axis=1)
            parts = []
            for j in range(3):
                weights = jnp.concatenate([kout[i, j] for i in range(3)], axis=0)
                parts.append(jnp.dot(lhs, weights, preferred_element_type=F32))
            x = xi[h + 1, pl.ds(f0, FB), :, CH:2 * CH].reshape(M, CH).astype(F32)
            y = from_left(parts[0]) + parts[1] + from_right(parts[2]) + skip[...] * x
            ob[h, pl.ds(f0, FB)] = y.astype(BF16).reshape(FB, W, CH)
            return 0

        lax.fori_loop(0, NB, block, 0)
        store = pltpu.make_async_copy(ob.at[h], out_hbm.at[:, h], osem.at[h])
        store.start()
        return store

    turn(sb, 1)
    row_tap(0, ci, 2)
    run((ro[0], 0))
    bx = x_to_z(1)
    row_tap(0, ci, 1)
    run((ro[1], 0), (ro[0], 1))
    row_tap(0, ci, 0)
    run((ro[2], 0), (ro[1], 1))
    bz = z_to_y(1)
    stores = [mix(1)]
    run((ro[2], 1), (ro[0], 2))
    from_y(1, bz, bx)
    lax.fori_loop(0, T // UN, adjoints, incoming[1].reshape(R, W, CH))
    turn(dcb, 0)
    row_tap(1, xi, 0)
    run((ri[0], 0), (ro[1], 2), (ro[2], 2), (ro[0], 3))
    row_tap(1, xi, 1)
    run((ri[1], 0), (ri[0], 1), (ro[1], 3), (ro[2], 3))
    row_tap(1, xi, 2)
    run((ri[2], 0), (ri[1], 1), (ro[0], 4), (ri[2], 1), (ri[0], 2), (ro[1], 4), (ro[2], 4))
    stores.append(mix(2))
    run((ri[1], 2), (ri[2], 2), (ri[0], 3), (ro[0], 5), (ro[1], 5), (ro[2], 5))
    halo_arrived(2)
    stores.append(mix(0))
    run((ri[1], 3), (ri[2], 3), (ri[0], 4), (ro[0], 6), (ro[1], 6), (ro[2], 6))
    stores.append(mix(3))
    run((ri[1], 4), (ri[2], 4), (ri[0], 5), (ro[0], 7), (ro[1], 7), (ro[2], 7))
    run((ri[1], 5), (ri[2], 5), (ri[0], 6))
    run((ri[1], 6), (ri[2], 6), (ri[0], 7), (ri[1], 7), (ri[2], 7))

    for n in range(3):
        halo_sent(n)
    for way in range(2):
        @pl.when(y_lo == way)
        def _():
            y_copy(way).wait_send()

    for store in stores:
        store.wait()
    for g in range(2):
        for q in range(3):
            out(g, q).wait()


def per_device(inputs, decays, in_kernel, out_kernel, skip, cotangent):
    cells_all = T * lax.axis_size("tm") * R * lax.axis_size("row") * W
    grad_scale = 1.0 / math.sqrt(cells_all)
    anywhere = pl.BlockSpec(memory_space=pl.ANY)
    vmem = pl.BlockSpec(memory_space=pltpu.VMEM)
    dma = pltpu.SemaphoreType.DMA
    V = pltpu.VMEM
    grad = jax.ShapeDtypeStruct((9, 2, 128, CH), BF16)
    outputs, in_grad, out_grad = pl.pallas_call(
        functools.partial(kernel, grad_scale),
        out_shape=(jax.ShapeDtypeStruct((T, R, W, CH), BF16), grad, grad),
        in_specs=[anywhere, vmem, anywhere, anywhere, vmem, anywhere],
        out_specs=(anywhere, anywhere, anywhere),
        scratch_shapes=[
            V((R + 2, T, W, 3 * CH), BF16),
            V((R + 2, T, W, 3 * CH), BF16),
            V((9 * CH, CH), BF16),
            V((3, 3, CH, CH), BF16),
            V((9 * CH, CH), BF16),
            V((R, T, W, CH), F32),
            V((R, T, W, CH), F32),
            V((R + 2, T, W, CH), BF16),
            V((R, T, W, CH), BF16),
            V((R, T, W, CH), BF16),
            V((T, CH), F32),
            V((2, 4, MSG, CH), F32),
            V((2, 4, MSG, CH), F32),
            V((2, 2, CELLS, CH), F32),
            V((2, CELLS, CH), F32),
            V((R, CH, T * W), BF16),
            V((2, 3, CH, 3 * CH), F32),
            V((2, 3, 384, CH), BF16),
            V((2, 3, 384, CH), BF16),
            V((384, CH), F32),
            V((LINE, 96, CH), F32),
            V((2, 3, 96, CH), F32),
            V((2, 3, LINE, 96, CH), BF16),
            V((2, 3, 3, 96, CH), BF16),
            V((2, 3, LINE) + CHUNK, F32),
            V((2, 3, 3) + CHUNK, F32),
            V((2, 3) + CHUNK, F32),
            V((2, 3, 3) + CHUNK, F32),
            V((2, 3, LINE, LINE) + CHUNK, BF16),
            V((2, 3, LINE, LINE) + CHUNK, BF16),
            V((2, 9, 2, 128, CH), BF16),
            dma((2, R)), dma((2,)), dma((R,)), dma((2, 3)),
            dma((3, 2)), dma((3, 2)),
            dma((2, 3)), dma((2, 4)), dma((2, 3)), dma((2, 4)), dma((2,)), dma((2,)),
            dma((2, 3)), dma((2, 3)), dma((2, 3)), dma((2, 3)), dma((2, 3)), dma((2, 3)), dma((2, 3)),
            dma((2, 3)), dma((2, 3)), dma((2, 3)), dma((2, 3)), dma((2, 3)), dma((2, 3)), dma((2, 3)),
        ],
        compiler_params=pltpu.CompilerParams(
            collective_id=0, has_side_effects=True, vmem_limit_bytes=62 * 1024 * 1024
        ),
    )(
        inputs.reshape(T, R, W, CH), decays, in_kernel.reshape(9 * CH, CH), out_kernel,
        skip.reshape(1, CH), cotangent.reshape(T, R, W, CH),
    )

    def whole(grad):
        return grad.reshape(3, 3, CH, CH).astype(F32)

    return outputs.reshape(inputs.shape), whole(in_grad), whole(out_grad)


def solution(mesh):
    return jax.shard_map(
        per_device,
        mesh=mesh,
        in_specs=(
            P(None, "tm", "row", None, None),
            P("tm", None),
            P(),
            P(),
            P(),
            P(None, "tm", "row", None, None),
        ),
        out_specs=(P(None, "tm", "row", None, None), P(), P()),
        check_vma=False,
    )
```

```python
import functools
import math

import jax
import jax.numpy as jnp
from jax import lax
from jax.experimental import pallas as pl
from jax.experimental.pallas import tpu as pltpu
from jax.sharding import PartitionSpec as P

MESH = pl.DeviceIdType.MESH
F32 = jnp.float32
BF16 = jnp.bfloat16

T = 64
R = 4
W = 16
CH = 256
FB = 32
NB = T // FB
M = FB * W
CELLS = R * W
MSG = CELLS + 8
LINE = 4
CHUNK = (48, 128)
ORDERS = (("x", "z", "y"), ("z", "y", "x"), ("y", "x", "z"))


def column(rows):
    return lax.broadcasted_iota(jnp.int32, (rows, CH), 0) & (W - 1)


def from_left(v):
    return jnp.where(column(v.shape[0]) == 0, 0.0, pltpu.roll(v, 1, 0))


def from_right(v):
    return jnp.where(column(v.shape[0]) == W - 1, 0.0, pltpu.roll(v, v.shape[0] - 1, 0))


def kernel(
    grad_scale,
    x_hbm, dec, kin_hbm, kout_hbm, skip, cot_hbm,
    out_hbm, gin_hbm, gout_hbm,
    xi, ci, kin, kout, ft, drv, adj, sb, ob, sc,
    rx, rz, ry, incoming,
    turned, acc, psend, precv, h1, h2, own, r15, s1, r1, c1, r2, c2, r3, agb, pgb, fb,
    lsem, wsem, osem, gsem,
    hsend, hrecv, xsend, xrecv, zsend, zrecv, ysend, yrecv,
    psem, prem, s1s, s1r, s2s, s2r, s3s, s3r, a2s, a2r, a1s, a1r, pgs, pgr,
):
    tm = lax.axis_index("tm")
    row = lax.axis_index("row")
    core = lax.rem(row, 2)
    y_lo = tm // 16
    pos = {"x": lax.rem(tm, 4), "z": lax.rem(tm // 4, 4), "y": (row // 2) * 2 + y_lo}

    def mate(axis, k):
        if axis == "x":
            return ((tm // 4) * 4 + k, row)
        if axis == "z":
            return (y_lo * 16 + k * 4 + lax.rem(tm, 4), row)
        return (lax.rem(k, 2) * 16 + lax.rem(tm, 16), (k // 2) * 2 + core)

    def mate_2(axis_1, k_1, axis_2, k_2):
        at = dict(pos)
        at[axis_1], at[axis_2] = k_1, k_2
        return (lax.rem(at["y"], 2) * 16 + at["z"] * 4 + at["x"], (at["y"] // 2) * 2 + core)

    def mates(axis):
        return [mate(axis, lax.rem(pos[axis] + d, LINE)) for d in (1, 2, 3)]

    pair = (tm, row + 1 - 2 * core)
    up = (tm, row - 1)
    down = (tm, row + 1)

    def remote(src, dst, ssem, rsem, device):
        return pltpu.make_async_remote_copy(
            src_ref=src, dst_ref=dst, send_sem=ssem, recv_sem=rsem,
            device_id=device, device_id_type=MESH,
        )

    barrier = pltpu.get_barrier_semaphore()

    def greet(device):
        pl.semaphore_signal(barrier, inc=1, device_id=device, device_id_type=MESH)

    @pl.when(row == 1)
    def _():
        greet(down)

    @pl.when(row == 2)
    def _():
        greet(up)

    greet(pair)
    for axis in ("y", "x", "z"):
        for device in mates(axis):
            greet(device)

    mid = pl.ds(CH, CH)
    loads = [
        [
            pltpu.make_async_copy(hbm.at[:, r], buf.at[r + 1, :, :, mid], lsem.at[n, r])
            for r in range(R)
        ]
        for n, (hbm, buf) in enumerate(((x_hbm, xi), (cot_hbm, ci)))
    ]
    load_kin = pltpu.make_async_copy(kin_hbm, kin, wsem.at[0])
    load_kout = pltpu.make_async_copy(kout_hbm, kout, wsem.at[1])
    for load in loads[0]:
        load.start()
    load_kin.start()
    load_kout.start()
    for load in loads[1]:
        load.start()

    for at, edge in ((0, 0), (3, R + 1)):
        @pl.when(row == at)
        def _():
            zero = jnp.zeros((T, W, CH), BF16)
            xi[edge, :, :, CH:2 * CH] = zero
            ci[edge, :, :, CH:2 * CH] = zero
            sb[edge] = zero

    d_all = dec[...]
    sc[...] = jnp.sqrt((1.0 - d_all) * (1.0 + d_all))

    @pl.when((row == 1) | (row == 2))
    def _():
        pl.semaphore_wait(barrier, 11)

    @pl.when((row == 0) | (row == 3))
    def _():
        pl.semaphore_wait(barrier, 10)

    def halo(n, way):
        if n == 2:
            src = sb.at[1] if way == 0 else sb.at[R]
            dst = sb.at[R + 1] if way == 0 else sb.at[0]
        else:
            hbm, buf = ((x_hbm, xi), (cot_hbm, ci))[n]
            src = hbm.at[:, 0] if way == 0 else hbm.at[:, R - 1]
            dst = buf.at[R + 1, :, :, mid] if way == 0 else buf.at[0, :, :, mid]
        return remote(src, dst, hsend.at[n, way], hrecv.at[n, way], up if way == 0 else down)

    def halo_start(n):
        @pl.when(row > 0)
        def _():
            halo(n, 0).start()

        @pl.when(row < 3)
        def _():
            halo(n, 1).start()

    def halo_arrived(n):
        @pl.when(row < 3)
        def _():
            halo(n, 0).wait_recv()

        @pl.when(row > 0)
        def _():
            halo(n, 1).wait_recv()

    def halo_sent(n):
        @pl.when(row > 0)
        def _():
            halo(n, 0).wait_send()

        @pl.when(row < 3)
        def _():
            halo(n, 1).wait_send()

    halo_start(0)
    halo_start(1)

    def widen(buf, r):
        def body(b, _):
            f0 = b * FB
            v = buf[r, pl.ds(f0, FB), :, CH:2 * CH].reshape(M, CH).astype(F32)
            buf[r, pl.ds(f0, FB), :, 0:CH] = from_left(v).astype(BF16).reshape(FB, W, CH)
            buf[r, pl.ds(f0, FB), :, 2 * CH:3 * CH] = from_right(v).astype(BF16).reshape(FB, W, CH)
            return 0

        lax.fori_loop(0, NB, body, 0)

    def conv(buf, weights, dst, first, stride, count):
        def body(n, _):
            h = first + (n // NB) * stride
            f0 = lax.rem(n, NB) * FB
            lhs = jnp.concatenate(
                [buf[h + i, pl.ds(f0, FB)].reshape(M, 3 * CH) for i in range(3)], axis=1
            )
            dst[h, pl.ds(f0, FB)] = jnp.dot(lhs, weights[...], preferred_element_type=F32).reshape(FB, W, CH)
            return 0

        lax.fori_loop(0, count * NB, body, 0)

    def turn_kernel():
        for i in range(3):
            for j in range(3):
                ft[(i * 3 + j) * CH:(i * 3 + j + 1) * CH, :] = kout[2 - i, 2 - j].T

    def widen_own(buf):
        def body(r, _):
            widen(buf, r)
            return 0

        lax.fori_loop(1, R + 1, body, 0)

    UN = 4

    def decay_at(t):
        return dec[pl.ds(t, 1), :]

    def ends_forward(n, carry):
        state, prod = carry
        for u in range(UN):
            t = n * UN + u
            d = decay_at(t)
            state = d * state + sc[pl.ds(t, 1), :] * drv[:, t]
            prod = prod * d
        return state, prod

    def ends_backward(n, v):
        for u in range(UN):
            t = T - 1 - (n * UN + u)
            v = decay_at(t) * (adj[:, t] + v)
        return v

    zero_state = jnp.zeros((R, W, CH), F32)

    def line(buf, way, axis, ssem, rsem, start):
        me = pos[axis]
        for d in (1, 2, 3):
            k = lax.rem(me + d, LINE)
            if start:
                remote(buf.at[way, me], buf.at[way, me], ssem.at[way, d - 1], rsem.at[way, me], mate(axis, k)).start()
            else:
                remote(buf.at[way, me], buf.at[way, k], ssem.at[way, d - 1], rsem.at[way, k], mate(axis, k)).wait()

    def fold(buf, way, me):
        before = jnp.zeros((CELLS, CH), F32)
        before_decay = jnp.ones((1, CH), F32)
        total = before
        total_decay = before_decay
        for p in (range(4) if way == 0 else range(3, -1, -1)):
            e, d = buf[way, p, 0:CELLS], buf[way, p, CELLS:CELLS + 1]
            takes = (me > p) if way == 0 else (me < p)
            before = jnp.where(takes, d * before + e, before)
            before_decay = jnp.where(takes, before_decay * d, before_decay)
            total = d * total + e
            total_decay = total_decay * d
        return before, before_decay, total, total_decay

    def put(buf, way, axis, total, decay):
        buf[way, pos[axis], 0:CELLS] = total
        buf[way, pos[axis], CELLS:MSG] = jnp.broadcast_to(decay, (8, CH))

    def y_copy(way):
        return remote(ry.at[way, 0], ry.at[way, 1], ysend.at[way], yrecv.at[way],
                      mate("y", (row // 2) * 2 + 1 - y_lo))

    def x_start(way, total, decay):
        put(rx, way, "x", total, decay)
        line(rx, way, "x", xsend, xrecv, True)

    def x_to_z(way):
        line(rx, way, "x", xsend, xrecv, False)
        before, before_decay, total, total_decay = fold(rx, way, pos["x"])
        put(rz, way, "z", total, total_decay)
        line(rz, way, "z", zsend, zrecv, True)
        return before, before_decay

    def z_to_y(way):
        line(rz, way, "z", zsend, zrecv, False)
        before, before_decay, total, _ = fold(rz, way, pos["z"])
        ry[way, 0] = total

        @pl.when(y_lo == way)
        def _():
            y_copy(way).start()

        return before, before_decay

    def from_y(way, z_side, x_side):
        z_before, z_decay = z_side
        x_before, x_decay = x_side
        incoming[way] = x_decay * z_before + x_before

        @pl.when(y_lo == 1 - way)
        def _():
            y_copy(way).wait_recv()
            incoming[way] = x_decay * (z_decay * ry[way, 1] + z_before) + x_before

    def states(n, state):
        for u in range(UN):
            t = n * UN + u
            state = decay_at(t) * state + sc[pl.ds(t, 1), :] * drv[:, t]
            sb[1:R + 1, t] = state.astype(BF16)
        return state

    for load in loads[0]:
        load.wait()
    widen_own(xi)
    load_kin.wait()
    conv(xi, kin, drv, 1, 1, 2)
    load_kout.wait()
    turn_kernel()
    for load in loads[1]:
        load.wait()
    widen_own(ci)
    halo_arrived(0)
    widen(xi, 0)
    widen(xi, R + 1)
    conv(xi, kin, drv, 0, 3, 2)
    end, decay = lax.fori_loop(0, T // UN, ends_forward, (zero_state, jnp.ones((1, CH), F32)))
    x_start(0, end.reshape(CELLS, CH), decay)

    conv(ci, ft, adj, 1, 1, 2)
    halo_arrived(1)
    widen(ci, 0)
    widen(ci, R + 1)
    fx = x_to_z(0)
    conv(ci, ft, adj, 0, 1, 1)
    fz = z_to_y(0)
    conv(ci, ft, adj, 3, 1, 1)
    lead = lax.fori_loop(0, T // UN, ends_backward, zero_state)
    x_start(1, lead.reshape(CELLS, CH), decay)
    from_y(0, fz, fx)
    lax.fori_loop(0, T // UN, states, incoming[0].reshape(R, W, CH))
    halo_start(2)

    def turn(field, at):
        for h in range(R):
            turned[:, h * T * W:(h + 1) * T * W] = field[h + at].astype(BF16).reshape(T * W, CH).T

    def row_tap(g, other, i):
        acc[g, i] = jnp.dot(
            turned[...], other[i:i + R].reshape(R * T * W, 3 * CH), preferred_element_type=F32
        )

    def adjoints(n, v):
        for u in range(UN):
            t = T - 1 - (n * UN + u)
            a = adj[:, t] + v
            drv[:, t] = sc[pl.ds(t, 1), :] * a
            v = decay_at(t) * a
        return v

    def part(g, q):
        pair_copy = remote(psend.at[g, q], precv.at[g, q], psem.at[g, q], prem.at[g, q], pair)

        def half(t, which):
            if g == 0:
                return acc[g, 2 - q, pl.ds(pl.multiple_of(which * 128, 128), 128), (2 - t) * CH:(3 - t) * CH]
            return acc[g, q, :, pl.ds(pl.multiple_of(t * CH + which * 128, 128), 128)].T

        def begin():
            for t in range(3):
                psend[g, q, t * 128:(t + 1) * 128] = half(t, 1 - core).astype(BF16)
            pair_copy.start()

        axis_1, axis_2, axis_3 = ORDERS[q]
        me_1, me_2 = pos[axis_1], pos[axis_2]

        def scatter():
            for t in range(3):
                h1[t * 128:(t + 1) * 128] = half(t, core)
            pair_copy.wait()
            for k in range(LINE):
                at = 96 * k
                v = h1[at:at + 96] + precv[g, q, at:at + 96].astype(F32)
                h2[k] = v
                s1[g, q, k] = v.astype(BF16)
            own[g, q] = h2[me_1]
            for d in (1, 2, 3):
                k = lax.rem(me_1 + d, LINE)
                remote(s1.at[g, q, k], r1.at[g, q, d - 1], s1s.at[g, q], s1r.at[g, q], mate(axis_1, k)).start()

        def second():
            remote(r1.at[g, q], r1.at[g, q], s1s.at[g, q], s1r.at[g, q], pair).wait()
            total = own[g, q]
            for d in range(3):
                total = total + r1[g, q, d].astype(F32)
            for k in range(LINE):
                c1[g, q, k] = total[48 * (k // 2):48 * (k // 2) + 48, 128 * (k % 2):128 * (k % 2) + 128]
            for d in (1, 2, 3):
                k = lax.rem(me_2 + d, LINE)
                remote(c1.at[g, q, k], r2.at[g, q, d - 1], s2s.at[g, q], s2r.at[g, q], mate(axis_2, k)).start()

        def cross():
            remote(r2.at[g, q], r2.at[g, q], s2s.at[g, q], s2r.at[g, q], pair).wait()
            c2[g, q] = c1[g, q, me_2] + r2[g, q, 0] + r2[g, q, 1] + r2[g, q, 2]
            for device, n in zip(mates(axis_3), range(3)):
                remote(c2.at[g, q], r3.at[g, q, n], s3s.at[g, q], s3r.at[g, q], device).start()

        def gather():
            remote(r3.at[g, q], r3.at[g, q], s3s.at[g, q], s3r.at[g, q], pair).wait()
            total = (c2[g, q] + r3[g, q, 1]) + (r3[g, q, 0] + r3[g, q, 2])
            mine = agb.at[g, q, me_1, me_2]
            mine[...] = (total * grad_scale).astype(BF16)
            for device in plane if wide else mates(axis_2):
                remote(mine, mine, a2s.at[g, q], a2r.at[g, q], device).start()

        wide = g == 1
        plane = [
            mate_2(axis_1, lax.rem(me_1 + d, LINE), axis_2, lax.rem(me_2 + e, LINE))
            for d in range(LINE) for e in range(LINE) if d + e > 0
        ]

        def share_wide():
            many = r15.at[...]
            remote(many, many, a2s.at[g, q], a2r.at[g, q], pair).wait()
            hand_over.start()

        def widen_out():
            three = agb.at[g, q, 0, pl.ds(0, 3)]
            remote(three, three, a2s.at[g, q], a2r.at[g, q], pair).wait()
            mine = agb.at[g, q, me_1]
            for device in mates(axis_1):
                remote(mine, mine, a1s.at[g, q], a1r.at[g, q], device).start()

        hand_over = remote(agb.at[g, q], pgb.at[g, q], pgs.at[g, q], pgr.at[g, q], pair)

        def share():
            three = agb.at[g, q, pl.ds(0, 3)]
            remote(three, three, a1s.at[g, q], a1r.at[g, q], pair).wait()
            hand_over.start()

        def unpack(buf, which):
            for k in range(LINE * LINE):
                at, lane = 48 * (k // 2), 128 * (k % 2)
                while at < 48 * (k // 2) + 48:
                    n = min(48 * (k // 2) + 48, (at // 128 + 1) * 128) - at
                    first = at - 48 * (k // 2)
                    fb[g, 3 * q + at // 128, which, at % 128:at % 128 + n, lane:lane + 128] = buf[g, q, k // LINE, k % LINE, first:first + n]
                    at += n

        def last():
            unpack(agb, core)
            hand_over.wait()
            unpack(pgb, 1 - core)
            out(g, q).start()

        if wide:
            return [begin, scatter, second, cross, gather, share_wide, lambda: None, last]
        return [begin, scatter, second, cross, gather, widen_out, share, last]

    def out(g, q):
        return pltpu.make_async_copy(
            fb.at[g, 3 * q:3 * q + 3], (gout_hbm, gin_hbm)[g].at[3 * q:3 * q + 3], gsem.at[g, q]
        )

    ro = [part(0, q) for q in range(3)]
    ri = [part(1, q) for q in range(3)]

    def run(*steps):
        for stages, n in steps:
            stages[n]()

    def mix(h):
        def block(b, _):
            f0 = b * FB
            lhs = jnp.concatenate([sb[h + i, pl.ds(f0, FB)].reshape(M, CH) for i in range(3)], axis=1)
            parts = []
            for j in range(3):
                weights = jnp.concatenate([kout[i, j] for i in range(3)], axis=0)
                parts.append(jnp.dot(lhs, weights, preferred_element_type=F32))
            x = xi[h + 1, pl.ds(f0, FB), :, CH:2 * CH].reshape(M, CH).astype(F32)
            y = from_left(parts[0]) + parts[1] + from_right(parts[2]) + skip[...] * x
            ob[h, pl.ds(f0, FB)] = y.astype(BF16).reshape(FB, W, CH)
            return 0

        lax.fori_loop(0, NB, block, 0)
        store = pltpu.make_async_copy(ob.at[h], out_hbm.at[:, h], osem.at[h])
        store.start()
        return store

    turn(sb, 1)
    row_tap(0, ci, 2)
    run((ro[0], 0))
    bx = x_to_z(1)
    row_tap(0, ci, 1)
    run((ro[1], 0), (ro[0], 1))
    row_tap(0, ci, 0)
    run((ro[2], 0), (ro[1], 1))
    bz = z_to_y(1)
    stores = [mix(1)]
    run((ro[2], 1), (ro[0], 2))
    from_y(1, bz, bx)
    lax.fori_loop(0, T // UN, adjoints, incoming[1].reshape(R, W, CH))
    turn(drv, 0)
    row_tap(1, xi, 0)
    run((ri[0], 0), (ro[1], 2), (ro[2], 2), (ro[0], 3))
    row_tap(1, xi, 1)
    run((ri[1], 0), (ri[0], 1), (ro[1], 3), (ro[2], 3))
    row_tap(1, xi, 2)
    run((ri[2], 0), (ri[1], 1), (ro[0], 4), (ri[2], 1), (ri[0], 2), (ro[1], 4), (ro[2], 4))
    stores.append(mix(2))
    run((ri[1], 2), (ri[2], 2), (ri[0], 3), (ro[0], 5), (ro[1], 5), (ro[2], 5))
    halo_arrived(2)
    stores.append(mix(0))
    run((ri[1], 3), (ri[2], 3), (ri[0], 4), (ro[0], 6), (ro[1], 6), (ro[2], 6))
    stores.append(mix(3))
    run((ri[1], 4), (ri[2], 4), (ri[0], 5), (ro[0], 7), (ro[1], 7), (ro[2], 7))
    run((ri[1], 5), (ri[2], 5), (ri[0], 6))
    run((ri[1], 6), (ri[2], 6), (ri[0], 7), (ri[1], 7), (ri[2], 7))

    for n in range(3):
        halo_sent(n)
    for way in range(2):
        @pl.when(y_lo == way)
        def _():
            y_copy(way).wait_send()

    for store in stores:
        store.wait()
    for g in range(2):
        for q in range(3):
            out(g, q).wait()


def finish(y_in, gin_in, gout_in, y_out, gin_out, gout_out, yb, gb, gf, ysem, gsem, ydone, gdone):
    grads = ((gout_in, gout_out), (gin_in, gin_out))
    y_loads = [pltpu.make_async_copy(y_in.at[n * FB:(n + 1) * FB], yb.at[n], ysem.at[n]) for n in range(NB)]
    y_stores = [pltpu.make_async_copy(yb.at[n], y_out.at[n * FB:(n + 1) * FB], ydone.at[n]) for n in range(NB)]
    g_loads = [[pltpu.make_async_copy(grads[g][0].at[3 * q:3 * q + 3], gb.at[g, q], gsem.at[g, q]) for q in range(3)] for g in range(2)]
    g_stores = [[pltpu.make_async_copy(gf.at[g, q], grads[g][1].at[3 * q:3 * q + 3], gdone.at[g, q]) for q in range(3)] for g in range(2)]
    for g in range(2):
        for q in range(3):
            g_loads[g][q].start()
    for load in y_loads:
        load.start()
    for g in range(2):
        for q in range(3):
            g_loads[g][q].wait()
            gf[g, q] = gb[g, q].astype(F32)
            g_stores[g][q].start()
    for load, store in zip(y_loads, y_stores):
        load.wait()
        store.start()
    for store in y_stores + g_stores[0] + g_stores[1]:
        store.wait()


def per_device(inputs, decays, in_kernel, out_kernel, skip, cotangent):
    cells_all = T * lax.axis_size("tm") * R * lax.axis_size("row") * W
    grad_scale = 1.0 / math.sqrt(cells_all)
    anywhere = pl.BlockSpec(memory_space=pl.ANY)
    vmem = pl.BlockSpec(memory_space=pltpu.VMEM)
    dma = pltpu.SemaphoreType.DMA
    V = pltpu.VMEM
    grad = jax.ShapeDtypeStruct((9, 2, 128, CH), BF16)
    outputs, in_grad, out_grad = pl.pallas_call(
        functools.partial(kernel, grad_scale),
        out_shape=(jax.ShapeDtypeStruct((T, R, W, CH), BF16), grad, grad),
        in_specs=[anywhere, vmem, anywhere, anywhere, vmem, anywhere],
        out_specs=(anywhere, anywhere, anywhere),
        scratch_shapes=[
            V((R + 2, T, W, 3 * CH), BF16),
            V((R + 2, T, W, 3 * CH), BF16),
            V((9 * CH, CH), BF16),
            V((3, 3, CH, CH), BF16),
            V((9 * CH, CH), BF16),
            V((R, T, W, CH), F32),
            V((R, T, W, CH), F32),
            V((R + 2, T, W, CH), BF16),
            V((R, T, W, CH), BF16),
            V((T, CH), F32),
            V((2, 4, MSG, CH), F32),
            V((2, 4, MSG, CH), F32),
            V((2, 2, CELLS, CH), F32),
            V((2, CELLS, CH), F32),
            V((CH, R * T * W), BF16),
            V((2, 3, CH, 3 * CH), F32),
            V((2, 3, 384, CH), BF16),
            V((2, 3, 384, CH), BF16),
            V((384, CH), F32),
            V((LINE, 96, CH), F32),
            V((2, 3, 96, CH), F32),
            V((15,) + CHUNK, BF16),
            V((2, 3, LINE, 96, CH), BF16),
            V((2, 3, 3, 96, CH), BF16),
            V((2, 3, LINE) + CHUNK, F32),
            V((2, 3, 3) + CHUNK, F32),
            V((2, 3) + CHUNK, F32),
            V((2, 3, 3) + CHUNK, F32),
            V((2, 3, LINE, LINE) + CHUNK, BF16),
            V((2, 3, LINE, LINE) + CHUNK, BF16),
            V((2, 9, 2, 128, CH), BF16),
            dma((2, R)), dma((2,)), dma((R,)), dma((2, 3)),
            dma((3, 2)), dma((3, 2)),
            dma((2, 3)), dma((2, 4)), dma((2, 3)), dma((2, 4)), dma((2,)), dma((2,)),
            dma((2, 3)), dma((2, 3)), dma((2, 3)), dma((2, 3)), dma((2, 3)), dma((2, 3)), dma((2, 3)),
            dma((2, 3)), dma((2, 3)), dma((2, 3)), dma((2, 3)), dma((2, 3)), dma((2, 3)), dma((2, 3)),
        ],
        compiler_params=pltpu.CompilerParams(
            collective_id=0, has_side_effects=True, vmem_limit_bytes=62 * 1024 * 1024
        ),
    )(
        inputs.reshape(T, R, W, CH), decays, in_kernel.reshape(9 * CH, CH), out_kernel,
        skip.reshape(1, CH), cotangent.reshape(T, R, W, CH),
    )

    grad = jax.ShapeDtypeStruct((9, 2, 128, CH), F32)
    outputs, in_grad, out_grad = pl.pallas_call(
        finish,
        out_shape=(jax.ShapeDtypeStruct((T, R, W, CH), BF16), grad, grad),
        in_specs=[pl.BlockSpec(memory_space=pltpu.HBM)] * 3,
        out_specs=(anywhere,) * 3,
        scratch_shapes=[
            V((NB, FB, R, W, CH), BF16),
            V((2, 3, 3, 2, 128, CH), BF16),
            V((2, 3, 3, 2, 128, CH), F32),
            dma((NB,)), dma((2, 3)), dma((NB,)), dma((2, 3)),
        ],
        compiler_params=pltpu.CompilerParams(vmem_limit_bytes=62 * 1024 * 1024),
    )(outputs, in_grad, out_grad)
    return outputs.reshape(inputs.shape), in_grad.reshape(3, 3, CH, CH), out_grad.reshape(3, 3, CH, CH)


def solution(mesh):
    return jax.shard_map(
        per_device,
        mesh=mesh,
        in_specs=(
            P(None, "tm", "row", None, None),
            P("tm", None),
            P(),
            P(),
            P(),
            P(None, "tm", "row", None, None),
        ),
        out_specs=(P(None, "tm", "row", None, None), P(), P()),
        check_vma=False,
    )
```

```python
import functools
import math

import jax
import jax.numpy as jnp
from jax import lax
from jax.experimental import pallas as pl
from jax.experimental.pallas import tpu as pltpu
from jax.sharding import PartitionSpec as P

MESH = pl.DeviceIdType.MESH
F32 = jnp.float32
BF16 = jnp.bfloat16

T = 64
R = 4
W = 16
CH = 256
FB = 32
NB = T // FB
M = FB * W
CELLS = R * W
MSG = CELLS + 8
LINE = 4
CHUNK = (48, 128)
ORDERS = (("x", "z", "y"), ("z", "y", "x"), ("y", "x", "z"))


def column(rows):
    return lax.broadcasted_iota(jnp.int32, (rows, CH), 0) & (W - 1)


def from_left(v):
    return jnp.where(column(v.shape[0]) == 0, 0.0, pltpu.roll(v, 1, 0))


def from_right(v):
    return jnp.where(column(v.shape[0]) == W - 1, 0.0, pltpu.roll(v, v.shape[0] - 1, 0))


def kernel(
    grad_scale,
    x_hbm, dec, kin_hbm, kout_hbm, skip, cot_hbm,
    out_hbm, gin_hbm, gout_hbm,
    xi, ci, kin, kout, ft, drv, adj, sb, ob, sc,
    rx, rz, ry, incoming,
    turned, acc, psend, precv, h1, h2, own, r15, s1, r1, c1, r2, c2, r3, agb, pgb, fb,
    lsem, wsem, osem, gsem,
    hsend, hrecv, xsend, xrecv, zsend, zrecv, ysend, yrecv,
    psem, prem, s1s, s1r, s2s, s2r, s3s, s3r, a2s, a2r, a1s, a1r, pgs, pgr,
):
    tm = lax.axis_index("tm")
    row = lax.axis_index("row")
    core = lax.rem(row, 2)
    y_lo = tm // 16
    pos = {"x": lax.rem(tm, 4), "z": lax.rem(tm // 4, 4), "y": (row // 2) * 2 + y_lo}

    def mate(axis, k):
        if axis == "x":
            return ((tm // 4) * 4 + k, row)
        if axis == "z":
            return (y_lo * 16 + k * 4 + lax.rem(tm, 4), row)
        return (lax.rem(k, 2) * 16 + lax.rem(tm, 16), (k // 2) * 2 + core)

    def mate_2(axis_1, k_1, axis_2, k_2):
        at = dict(pos)
        at[axis_1], at[axis_2] = k_1, k_2
        return (lax.rem(at["y"], 2) * 16 + at["z"] * 4 + at["x"], (at["y"] // 2) * 2 + core)

    def mates(axis):
        return [mate(axis, lax.rem(pos[axis] + d, LINE)) for d in (1, 2, 3)]

    pair = (tm, row + 1 - 2 * core)
    up = (tm, row - 1)
    down = (tm, row + 1)

    def remote(src, dst, ssem, rsem, device):
        return pltpu.make_async_remote_copy(
            src_ref=src, dst_ref=dst, send_sem=ssem, recv_sem=rsem,
            device_id=device, device_id_type=MESH,
        )

    barrier = pltpu.get_barrier_semaphore()

    def greet(device):
        pl.semaphore_signal(barrier, inc=1, device_id=device, device_id_type=MESH)

    @pl.when(row == 1)
    def _():
        greet(down)

    @pl.when(row == 2)
    def _():
        greet(up)

    greet(pair)
    for axis in ("y", "x", "z"):
        for device in mates(axis):
            greet(device)

    mid = pl.ds(CH, CH)
    loads = [
        [
            pltpu.make_async_copy(hbm.at[:, r], buf.at[r + 1, :, :, mid], lsem.at[n, r])
            for r in range(R)
        ]
        for n, (hbm, buf) in enumerate(((x_hbm, xi), (cot_hbm, ci)))
    ]
    load_kin = pltpu.make_async_copy(kin_hbm, kin, wsem.at[0])
    load_kout = pltpu.make_async_copy(kout_hbm, kout, wsem.at[1])
    for load in loads[0]:
        load.start()
    load_kin.start()
    load_kout.start()
    for load in loads[1]:
        load.start()

    for at, edge in ((0, 0), (3, R + 1)):
        @pl.when(row == at)
        def _():
            zero = jnp.zeros((T, W, CH), BF16)
            xi[edge, :, :, CH:2 * CH] = zero
            ci[edge, :, :, CH:2 * CH] = zero
            sb[edge] = zero

    d_all = dec[...]
    sc[...] = jnp.sqrt((1.0 - d_all) * (1.0 + d_all))

    @pl.when((row == 1) | (row == 2))
    def _():
        pl.semaphore_wait(barrier, 11)

    @pl.when((row == 0) | (row == 3))
    def _():
        pl.semaphore_wait(barrier, 10)

    def halo(n, way):
        if n == 2:
            src = sb.at[1] if way == 0 else sb.at[R]
            dst = sb.at[R + 1] if way == 0 else sb.at[0]
        else:
            hbm, buf = ((x_hbm, xi), (cot_hbm, ci))[n]
            src = hbm.at[:, 0] if way == 0 else hbm.at[:, R - 1]
            dst = buf.at[R + 1, :, :, mid] if way == 0 else buf.at[0, :, :, mid]
        return remote(src, dst, hsend.at[n, way], hrecv.at[n, way], up if way == 0 else down)

    def halo_start(n):
        @pl.when(row > 0)
        def _():
            halo(n, 0).start()

        @pl.when(row < 3)
        def _():
            halo(n, 1).start()

    def halo_arrived(n):
        @pl.when(row < 3)
        def _():
            halo(n, 0).wait_recv()

        @pl.when(row > 0)
        def _():
            halo(n, 1).wait_recv()

    def halo_sent(n):
        @pl.when(row > 0)
        def _():
            halo(n, 0).wait_send()

        @pl.when(row < 3)
        def _():
            halo(n, 1).wait_send()

    halo_start(0)
    halo_start(1)

    def widen(buf, r):
        def body(b, _):
            f0 = b * FB
            v = buf[r, pl.ds(f0, FB), :, CH:2 * CH].reshape(M, CH).astype(F32)
            buf[r, pl.ds(f0, FB), :, 0:CH] = from_left(v).astype(BF16).reshape(FB, W, CH)
            buf[r, pl.ds(f0, FB), :, 2 * CH:3 * CH] = from_right(v).astype(BF16).reshape(FB, W, CH)
            return 0

        lax.fori_loop(0, NB, body, 0)

    def conv(buf, weights, dst, first, stride, count):
        def body(n, _):
            h = first + (n // NB) * stride
            f0 = lax.rem(n, NB) * FB
            lhs = jnp.concatenate(
                [buf[h + i, pl.ds(f0, FB)].reshape(M, 3 * CH) for i in range(3)], axis=1
            )
            dst[h, pl.ds(f0, FB)] = jnp.dot(lhs, weights[...], preferred_element_type=F32).reshape(FB, W, CH)
            return 0

        lax.fori_loop(0, count * NB, body, 0)

    def turn_kernel():
        for i in range(3):
            for j in range(3):
                ft[(i * 3 + j) * CH:(i * 3 + j + 1) * CH, :] = kout[2 - i, 2 - j].T

    def widen_own(buf):
        def body(r, _):
            widen(buf, r)
            return 0

        lax.fori_loop(1, R + 1, body, 0)

    UN = 8

    def decay_at(t):
        return dec[pl.ds(t, 1), :]

    def ends_forward(n, carry):
        state, prod = carry
        for u in range(UN):
            t = n * UN + u
            d = decay_at(t)
            state = d * state + sc[pl.ds(t, 1), :] * drv[:, t]
            prod = prod * d
        return state, prod

    def ends_backward(n, v):
        for u in range(UN):
            t = T - 1 - (n * UN + u)
            v = decay_at(t) * (adj[:, t] + v)
        return v

    zero_state = jnp.zeros((R, W, CH), F32)

    def line(buf, way, axis, ssem, rsem, start):
        me = pos[axis]
        for d in (1, 2, 3):
            k = lax.rem(me + d, LINE)
            if start:
                remote(buf.at[way, me], buf.at[way, me], ssem.at[way, d - 1], rsem.at[way, me], mate(axis, k)).start()
            else:
                remote(buf.at[way, me], buf.at[way, k], ssem.at[way, d - 1], rsem.at[way, k], mate(axis, k)).wait()

    def fold(buf, way, me):
        before = jnp.zeros((CELLS, CH), F32)
        before_decay = jnp.ones((1, CH), F32)
        total = before
        total_decay = before_decay
        for p in (range(4) if way == 0 else range(3, -1, -1)):
            e, d = buf[way, p, 0:CELLS], buf[way, p, CELLS:CELLS + 1]
            takes = (me > p) if way == 0 else (me < p)
            before = jnp.where(takes, d * before + e, before)
            before_decay = jnp.where(takes, before_decay * d, before_decay)
            total = d * total + e
            total_decay = total_decay * d
        return before, before_decay, total, total_decay

    def put(buf, way, axis, total, decay):
        buf[way, pos[axis], 0:CELLS] = total
        buf[way, pos[axis], CELLS:MSG] = jnp.broadcast_to(decay, (8, CH))

    def y_copy(way):
        return remote(ry.at[way, 0], ry.at[way, 1], ysend.at[way], yrecv.at[way],
                      mate("y", (row // 2) * 2 + 1 - y_lo))

    def x_start(way, total, decay):
        put(rx, way, "x", total, decay)
        line(rx, way, "x", xsend, xrecv, True)

    def x_to_z(way):
        line(rx, way, "x", xsend, xrecv, False)
        before, before_decay, total, total_decay = fold(rx, way, pos["x"])
        put(rz, way, "z", total, total_decay)
        line(rz, way, "z", zsend, zrecv, True)
        return before, before_decay

    def z_to_y(way):
        line(rz, way, "z", zsend, zrecv, False)
        before, before_decay, total, _ = fold(rz, way, pos["z"])
        ry[way, 0] = total

        @pl.when(y_lo == way)
        def _():
            y_copy(way).start()

        return before, before_decay

    def from_y(way, z_side, x_side):
        z_before, z_decay = z_side
        x_before, x_decay = x_side
        incoming[way] = x_decay * z_before + x_before

        @pl.when(y_lo == 1 - way)
        def _():
            y_copy(way).wait_recv()
            incoming[way] = x_decay * (z_decay * ry[way, 1] + z_before) + x_before

    def states(n, state):
        for u in range(UN):
            t = n * UN + u
            state = decay_at(t) * state + sc[pl.ds(t, 1), :] * drv[:, t]
            sb[1:R + 1, t] = state.astype(BF16)
        return state

    for load in loads[0]:
        load.wait()
    widen_own(xi)
    load_kin.wait()
    conv(xi, kin, drv, 1, 1, 2)
    load_kout.wait()
    turn_kernel()
    for load in loads[1]:
        load.wait()
    widen_own(ci)
    halo_arrived(0)
    widen(xi, 0)
    widen(xi, R + 1)
    conv(xi, kin, drv, 0, 3, 2)
    end, decay = lax.fori_loop(0, T // UN, ends_forward, (zero_state, jnp.ones((1, CH), F32)))
    x_start(0, end.reshape(CELLS, CH), decay)

    conv(ci, ft, adj, 1, 1, 2)
    halo_arrived(1)
    widen(ci, 0)
    widen(ci, R + 1)
    fx = x_to_z(0)
    conv(ci, ft, adj, 0, 1, 1)
    conv(ci, ft, adj, 3, 1, 1)
    lead = lax.fori_loop(0, T // UN, ends_backward, zero_state)
    x_start(1, lead.reshape(CELLS, CH), decay)
    fz = z_to_y(0)
    from_y(0, fz, fx)
    lax.fori_loop(0, T // UN, states, incoming[0].reshape(R, W, CH))
    halo_start(2)

    def turn(field, at):
        for h in range(R):
            turned[:, h * T * W:(h + 1) * T * W] = field[h + at].astype(BF16).reshape(T * W, CH).T

    def row_tap(g, other, i):
        acc[g, i] = jnp.dot(
            turned[...], other[i:i + R].reshape(R * T * W, 3 * CH), preferred_element_type=F32
        )

    def adjoints(n, v):
        for u in range(UN):
            t = T - 1 - (n * UN + u)
            a = adj[:, t] + v
            drv[:, t] = sc[pl.ds(t, 1), :] * a
            v = decay_at(t) * a
        return v

    def part(g, q):
        pair_copy = remote(psend.at[g, q], precv.at[g, q], psem.at[g, q], prem.at[g, q], pair)

        def half(t, which):
            if g == 0:
                return acc[g, 2 - q, pl.ds(pl.multiple_of(which * 128, 128), 128), (2 - t) * CH:(3 - t) * CH]
            return acc[g, q, :, pl.ds(pl.multiple_of(t * CH + which * 128, 128), 128)].T

        def begin():
            for t in range(3):
                psend[g, q, t * 128:(t + 1) * 128] = half(t, 1 - core).astype(BF16)
            pair_copy.start()

        axis_1, axis_2, axis_3 = ORDERS[q]
        me_1, me_2 = pos[axis_1], pos[axis_2]

        def scatter():
            for t in range(3):
                h1[t * 128:(t + 1) * 128] = half(t, core)
            pair_copy.wait()
            for k in range(LINE):
                at = 96 * k
                v = h1[at:at + 96] + precv[g, q, at:at + 96].astype(F32)
                h2[k] = v
                s1[g, q, k] = v.astype(BF16)
            own[g, q] = h2[me_1]
            for d in (1, 2, 3):
                k = lax.rem(me_1 + d, LINE)
                remote(s1.at[g, q, k], r1.at[g, q, d - 1], s1s.at[g, q], s1r.at[g, q], mate(axis_1, k)).start()

        def second():
            remote(r1.at[g, q], r1.at[g, q], s1s.at[g, q], s1r.at[g, q], pair).wait()
            total = own[g, q]
            for d in range(3):
                total = total + r1[g, q, d].astype(F32)
            for k in range(LINE):
                c1[g, q, k] = total[48 * (k // 2):48 * (k // 2) + 48, 128 * (k % 2):128 * (k % 2) + 128]
            for d in (1, 2, 3):
                k = lax.rem(me_2 + d, LINE)
                remote(c1.at[g, q, k], r2.at[g, q, d - 1], s2s.at[g, q], s2r.at[g, q], mate(axis_2, k)).start()

        def cross():
            remote(r2.at[g, q], r2.at[g, q], s2s.at[g, q], s2r.at[g, q], pair).wait()
            c2[g, q] = c1[g, q, me_2] + r2[g, q, 0] + r2[g, q, 1] + r2[g, q, 2]
            for device, n in zip(mates(axis_3), range(3)):
                remote(c2.at[g, q], r3.at[g, q, n], s3s.at[g, q], s3r.at[g, q], device).start()

        def gather():
            remote(r3.at[g, q], r3.at[g, q], s3s.at[g, q], s3r.at[g, q], pair).wait()
            total = (c2[g, q] + r3[g, q, 1]) + (r3[g, q, 0] + r3[g, q, 2])
            mine = agb.at[g, q, me_1, me_2]
            mine[...] = (total * grad_scale).astype(BF16)
            for device in plane if wide else mates(axis_2):
                remote(mine, mine, a2s.at[g, q], a2r.at[g, q], device).start()

        wide = g == 1
        plane = [
            mate_2(axis_1, lax.rem(me_1 + d, LINE), axis_2, lax.rem(me_2 + e, LINE))
            for d in range(LINE) for e in range(LINE) if d + e > 0
        ]

        def share_wide():
            many = r15.at[...]
            remote(many, many, a2s.at[g, q], a2r.at[g, q], pair).wait()
            hand_over.start()

        def widen_out():
            three = agb.at[g, q, 0, pl.ds(0, 3)]
            remote(three, three, a2s.at[g, q], a2r.at[g, q], pair).wait()
            mine = agb.at[g, q, me_1]
            for device in mates(axis_1):
                remote(mine, mine, a1s.at[g, q], a1r.at[g, q], device).start()

        hand_over = remote(agb.at[g, q], pgb.at[g, q], pgs.at[g, q], pgr.at[g, q], pair)

        def share():
            three = agb.at[g, q, pl.ds(0, 3)]
            remote(three, three, a1s.at[g, q], a1r.at[g, q], pair).wait()
            hand_over.start()

        def unpack(buf, which):
            for k in range(LINE * LINE):
                at, lane = 48 * (k // 2), 128 * (k % 2)
                while at < 48 * (k // 2) + 48:
                    n = min(48 * (k // 2) + 48, (at // 128 + 1) * 128) - at
                    first = at - 48 * (k // 2)
                    fb[g, 3 * q + at // 128, which, at % 128:at % 128 + n, lane:lane + 128] = buf[g, q, k // LINE, k % LINE, first:first + n]
                    at += n

        def last():
            unpack(agb, core)
            hand_over.wait()
            unpack(pgb, 1 - core)
            out(g, q).start()

        if wide:
            return [begin, scatter, second, cross, gather, share_wide, lambda: None, last]
        return [begin, scatter, second, cross, gather, widen_out, share, last]

    def out(g, q):
        return pltpu.make_async_copy(
            fb.at[g, 3 * q:3 * q + 3], (gout_hbm, gin_hbm)[g].at[3 * q:3 * q + 3], gsem.at[g, q]
        )

    ro = [part(0, q) for q in range(3)]
    ri = [part(1, q) for q in range(3)]

    def run(*steps):
        for stages, n in steps:
            stages[n]()

    def mix(h):
        def block(b, _):
            f0 = b * FB
            lhs = jnp.concatenate([sb[h + i, pl.ds(f0, FB)].reshape(M, CH) for i in range(3)], axis=1)
            parts = []
            for j in range(3):
                weights = jnp.concatenate([kout[i, j] for i in range(3)], axis=0)
                parts.append(jnp.dot(lhs, weights, preferred_element_type=F32))
            x = xi[h + 1, pl.ds(f0, FB), :, CH:2 * CH].reshape(M, CH).astype(F32)
            y = from_left(parts[0]) + parts[1] + from_right(parts[2]) + skip[...] * x
            ob[h, pl.ds(f0, FB)] = y.astype(BF16).reshape(FB, W, CH)
            return 0

        lax.fori_loop(0, NB, block, 0)
        store = pltpu.make_async_copy(ob.at[h], out_hbm.at[:, h], osem.at[h])
        store.start()
        return store

    bx = x_to_z(1)
    turn(sb, 1)
    row_tap(0, ci, 2)
    run((ro[0], 0))
    row_tap(0, ci, 1)
    run((ro[1], 0), (ro[0], 1))
    row_tap(0, ci, 0)
    bz = z_to_y(1)
    run((ro[2], 0), (ro[1], 1))
    stores = [mix(1)]
    run((ro[2], 1), (ro[0], 2))
    from_y(1, bz, bx)
    lax.fori_loop(0, T // UN, adjoints, incoming[1].reshape(R, W, CH))
    turn(drv, 0)
    row_tap(1, xi, 0)
    run((ri[0], 0), (ro[1], 2), (ro[2], 2), (ro[0], 3))
    row_tap(1, xi, 1)
    run((ri[1], 0), (ri[0], 1), (ro[1], 3), (ro[2], 3))
    row_tap(1, xi, 2)
    run((ri[2], 0), (ri[1], 1), (ro[0], 4), (ri[2], 1), (ri[0], 2), (ro[1], 4), (ro[2], 4))
    stores.append(mix(2))
    run((ri[1], 2), (ri[2], 2), (ri[0], 3), (ro[0], 5), (ro[1], 5), (ro[2], 5))
    halo_arrived(2)
    stores.append(mix(0))
    run((ri[1], 3), (ri[2], 3), (ri[0], 4), (ro[0], 6), (ro[1], 6), (ro[2], 6))
    stores.append(mix(3))
    run((ri[1], 4), (ri[2], 4), (ri[0], 5), (ro[0], 7), (ro[1], 7), (ro[2], 7))
    run((ri[1], 5), (ri[2], 5), (ri[0], 6))
    run((ri[1], 6), (ri[2], 6), (ri[0], 7), (ri[1], 7), (ri[2], 7))

    for n in range(3):
        halo_sent(n)
    for way in range(2):
        @pl.when(y_lo == way)
        def _():
            y_copy(way).wait_send()

    for store in stores:
        store.wait()
    for g in range(2):
        for q in range(3):
            out(g, q).wait()


def finish(y_in, gin_in, gout_in, y_out, gin_out, gout_out, yb, gb, gf, ysem, gsem, ydone, gdone):
    grads = ((gout_in, gout_out), (gin_in, gin_out))
    y_loads = [pltpu.make_async_copy(y_in.at[n * FB:(n + 1) * FB], yb.at[n], ysem.at[n]) for n in range(NB)]
    y_stores = [pltpu.make_async_copy(yb.at[n], y_out.at[n * FB:(n + 1) * FB], ydone.at[n]) for n in range(NB)]
    g_loads = [[pltpu.make_async_copy(grads[g][0].at[3 * q:3 * q + 3], gb.at[g, q], gsem.at[g, q]) for q in range(3)] for g in range(2)]
    g_stores = [[pltpu.make_async_copy(gf.at[g, q], grads[g][1].at[3 * q:3 * q + 3], gdone.at[g, q]) for q in range(3)] for g in range(2)]
    for g in range(2):
        for q in range(3):
            g_loads[g][q].start()
    for load in y_loads:
        load.start()
    for g in range(2):
        for q in range(3):
            g_loads[g][q].wait()
            gf[g, q] = gb[g, q].astype(F32)
            g_stores[g][q].start()
    for load, store in zip(y_loads, y_stores):
        load.wait()
        store.start()
    for store in y_stores + g_stores[0] + g_stores[1]:
        store.wait()


def per_device(inputs, decays, in_kernel, out_kernel, skip, cotangent):
    cells_all = T * lax.axis_size("tm") * R * lax.axis_size("row") * W
    grad_scale = 1.0 / math.sqrt(cells_all)
    anywhere = pl.BlockSpec(memory_space=pl.ANY)
    vmem = pl.BlockSpec(memory_space=pltpu.VMEM)
    dma = pltpu.SemaphoreType.DMA
    V = pltpu.VMEM
    grad = jax.ShapeDtypeStruct((9, 2, 128, CH), BF16)
    outputs, in_grad, out_grad = pl.pallas_call(
        functools.partial(kernel, grad_scale),
        out_shape=(jax.ShapeDtypeStruct((T, R, W, CH), BF16), grad, grad),
        in_specs=[anywhere, vmem, anywhere, anywhere, vmem, anywhere],
        out_specs=(anywhere, anywhere, anywhere),
        scratch_shapes=[
            V((R + 2, T, W, 3 * CH), BF16),
            V((R + 2, T, W, 3 * CH), BF16),
            V((9 * CH, CH), BF16),
            V((3, 3, CH, CH), BF16),
            V((9 * CH, CH), BF16),
            V((R, T, W, CH), F32),
            V((R, T, W, CH), F32),
            V((R + 2, T, W, CH), BF16),
            V((R, T, W, CH), BF16),
            V((T, CH), F32),
            V((2, 4, MSG, CH), F32),
            V((2, 4, MSG, CH), F32),
            V((2, 2, CELLS, CH), F32),
            V((2, CELLS, CH), F32),
            V((CH, R * T * W), BF16),
            V((2, 3, CH, 3 * CH), F32),
            V((2, 3, 384, CH), BF16),
            V((2, 3, 384, CH), BF16),
            V((384, CH), F32),
            V((LINE, 96, CH), F32),
            V((2, 3, 96, CH), F32),
            V((15,) + CHUNK, BF16),
            V((2, 3, LINE, 96, CH), BF16),
            V((2, 3, 3, 96, CH), BF16),
            V((2, 3, LINE) + CHUNK, F32),
            V((2, 3, 3) + CHUNK, F32),
            V((2, 3) + CHUNK, F32),
            V((2, 3, 3) + CHUNK, F32),
            V((2, 3, LINE, LINE) + CHUNK, BF16),
            V((2, 3, LINE, LINE) + CHUNK, BF16),
            V((2, 9, 2, 128, CH), BF16),
            dma((2, R)), dma((2,)), dma((R,)), dma((2, 3)),
            dma((3, 2)), dma((3, 2)),
            dma((2, 3)), dma((2, 4)), dma((2, 3)), dma((2, 4)), dma((2,)), dma((2,)),
            dma((2, 3)), dma((2, 3)), dma((2, 3)), dma((2, 3)), dma((2, 3)), dma((2, 3)), dma((2, 3)),
            dma((2, 3)), dma((2, 3)), dma((2, 3)), dma((2, 3)), dma((2, 3)), dma((2, 3)), dma((2, 3)),
        ],
        compiler_params=pltpu.CompilerParams(
            collective_id=0, has_side_effects=True, vmem_limit_bytes=62 * 1024 * 1024
        ),
    )(
        inputs.reshape(T, R, W, CH), decays, in_kernel.reshape(9 * CH, CH), out_kernel,
        skip.reshape(1, CH), cotangent.reshape(T, R, W, CH),
    )

    grad = jax.ShapeDtypeStruct((9, 2, 128, CH), F32)
    outputs, in_grad, out_grad = pl.pallas_call(
        finish,
        out_shape=(jax.ShapeDtypeStruct((T, R, W, CH), BF16), grad, grad),
        in_specs=[pl.BlockSpec(memory_space=pltpu.HBM)] * 3,
        out_specs=(anywhere,) * 3,
        scratch_shapes=[
            V((NB, FB, R, W, CH), BF16),
            V((2, 3, 3, 2, 128, CH), BF16),
            V((2, 3, 3, 2, 128, CH), F32),
            dma((NB,)), dma((2, 3)), dma((NB,)), dma((2, 3)),
        ],
        compiler_params=pltpu.CompilerParams(vmem_limit_bytes=62 * 1024 * 1024),
    )(outputs, in_grad, out_grad)
    return outputs.reshape(inputs.shape), in_grad.reshape(3, 3, CH, CH), out_grad.reshape(3, 3, CH, CH)


def solution(mesh):
    return jax.shard_map(
        per_device,
        mesh=mesh,
        in_specs=(
            P(None, "tm", "row", None, None),
            P("tm", None),
            P(),
            P(),
            P(),
            P(None, "tm", "row", None, None),
        ),
        out_specs=(P(None, "tm", "row", None, None), P(), P()),
        check_vma=False,
    )
```
